32 devices in a mesh: cam: 2 (over core), tile: 16 (over z, y, x).
Axes of the slice: x: 2, y: 2, z: 4, core: 2. Of those that a mesh axis runs over, the one named last changes fastest.
Arguments:
- queries: bfloat16 [4096, 256], P('tile'), as said below
- keys: bfloat16 [2048, 256], P(('cam', 'tile')), as said below
- values: bfloat16 [2048, 256], P(('cam', 'tile')), may hold values from -6 to 6
- grad_out: bfloat16 [4096, 256], P('tile'), may hold values from -6 to 6
- visible: int32 [32, 64], P('tile', 'cam'), may hold values from 0 to 1, as said below
- counts: int32 [64], P('cam'), may hold values from 2 to 32
Outputs:
- grad_queries: bfloat16 [4096, 256], P('tile')
- grad_keys: bfloat16 [2048, 256], P(('cam', 'tile'))
- grad_values: bfloat16 [2048, 256], P(('cam', 'tile'))
The draws below stay inside these ranges and needn't reach their ends.
Inputs may be any that keep to these rules, and one draw needn't show every extreme that they name: Every tile has at least one visible block. `queries`: projected query features. `keys`: projected key features.
All inputs are finite; a program needn't handle non-finite values.
Results may differ from the reference program's by a relative error of at most 0.0052.
Values may be sent and summed in bfloat16 or wider, within the bound.
No kernel may reach another device: no remote copies, remote signals or barrier semaphores. Data moves between devices by JAX's collectives and lax.ppermute only.
A program may use at most 128 MiB of HBM per device.

```python
import math
import jax
import jax.numpy as jnp
from jax import lax

C = 256
H = 8
HD = 32
TQ = 128
KB = 32
TILES = 32
QUERIES = 4096
KEYS = 2048
KBLOCKS = 64


def camera_keys(key):
    base = jax.random.fold_in(key, 101)
    return jax.random.normal(base, (KEYS, C), jnp.float32)


def forced_blocks(key):
    return jax.random.randint(jax.random.fold_in(key, 202), (TILES,), 0, KBLOCKS)


def draw_keys(key, part):
    return camera_keys(key).astype(jnp.bfloat16)


def draw_queries(key, part):
    drawn = jax.random.normal(jax.random.fold_in(key, 303), (QUERIES, C), jnp.float32)
    return drawn.astype(jnp.bfloat16)


def draw_visible(key, part):
    coin = jax.random.randint(jax.random.fold_in(key, 404), (TILES, KBLOCKS), 0, 2)
    forced = forced_blocks(key)
    hit = (jnp.arange(KBLOCKS, dtype=jnp.int32)[None, :] == forced[:, None]).astype(jnp.int32)
    return jnp.maximum(coin, hit).astype(jnp.int32)


def plant(values, own_key, least, top_value):
    extent = values.shape
    index_at = [jax.random.randint(jax.random.fold_in(own_key, axis), (), 0, extent[axis]) for axis in range(len(extent))]
    values = values.at[tuple(index_at)].set(least)
    longest = extent.index(max(extent))
    index_at[longest] = (index_at[longest] + 1) % extent[longest]
    return values.at[tuple(index_at)].set(top_value)


def steps_of(own_key, dims, cuts, least, largest):
    def one(dim, parts):
        draws = jax.random.uniform(jax.random.fold_in(jax.random.fold_in(own_key, 6), dim), (parts,), jnp.float32, least / len(cuts), largest / len(cuts))
        return jnp.repeat(jnp.exp(draws), dims[dim] // parts).reshape((-1,) + (1,) * (len(dims) - dim - 1))

    factor_of = one(*cuts[0])
    for cut in cuts[1:]:
        factor_of = factor_of * one(*cut)
    return factor_of


def gaussian(rng, dims, deviation, bound, split=(), held_as=jnp.bfloat16):
    drawn = jax.random.normal(rng, dims, jnp.float32) * deviation
    if len(split) > 0:
        drawn = steps_of(rng, dims, split, -0.22, 0.18) * drawn
    return jnp.clip(drawn, min=-bound, max=bound).astype(held_as)


def setup_inputs(seed: int = 0) -> dict:
    streams_of = jax.random.split(jax.random.key(seed), 7)
    return {
        "queries": draw_queries(jax.random.fold_in(streams_of[6], 71), 0),
        "keys": draw_keys(jax.random.fold_in(streams_of[6], 71), 0),
        "values": gaussian(streams_of[2], (KEYS, C), 1.0, 6.0, ((0, 32),)),
        "grad_out": gaussian(streams_of[3], (QUERIES, C), 1.0, 6.0, ((0, 16),)),
        "visible": draw_visible(jax.random.fold_in(streams_of[6], 71), 0),
        "counts": plant(jax.random.randint(streams_of[5], (KBLOCKS,), 2, KB + 1), jax.random.fold_in(streams_of[5], 1), 2, KB).astype(jnp.int32),
    }


def reference(queries, keys, values, grad_out, visible, counts):
    scale = 1.0 / math.sqrt(HD)
    key_index = jnp.arange(KEYS, dtype=jnp.int32)
    block_of = key_index // KB
    key_valid = key_index % KB < counts[block_of]
    key_heads = keys.astype(jnp.float32).reshape(KEYS, H, HD)
    value_heads = values.astype(jnp.float32).reshape(KEYS, H, HD)

    def tile_step(carry, tile_index):
        grad_k, grad_v = carry
        start = (tile_index * TQ).astype(jnp.int32)
        query_tile = lax.dynamic_slice_in_dim(queries, start, TQ, 0).astype(jnp.float32).reshape(TQ, H, HD)
        grad_tile = lax.dynamic_slice_in_dim(grad_out, start, TQ, 0).astype(jnp.float32).reshape(TQ, H, HD)
        vis_row = lax.dynamic_index_in_dim(visible, tile_index, 0, keepdims=False)
        allowed = ((vis_row[block_of] == 1) & key_valid)[None, None, :]
        scores = jnp.einsum('qhd,khd->hqk', query_tile, key_heads) * scale
        top = lax.optimization_barrier(jnp.max(jnp.where(allowed, scores, -1e+30), axis=-1))
        total = lax.optimization_barrier(jnp.sum(jnp.where(allowed, jnp.exp(scores - top[..., None]), 0.0), axis=-1))
        lse = top + jnp.log(total)
        probs = jnp.where(allowed, jnp.exp(scores - lse[..., None]), 0.0)
        dprobs = jnp.einsum('qhd,khd->hqk', grad_tile, value_heads)
        delta = lax.optimization_barrier(jnp.sum(probs * dprobs, axis=-1))
        dscores = probs * (dprobs - delta[..., None])
        probs_b = probs.astype(jnp.bfloat16).astype(jnp.float32)
        dscores_b = dscores.astype(jnp.bfloat16).astype(jnp.float32)
        grad_q = jnp.einsum('hqk,khd->qhd', dscores_b, key_heads) * scale
        grad_k = grad_k + jnp.einsum('hqk,qhd->khd', dscores_b, query_tile) * scale
        grad_v = grad_v + jnp.einsum('hqk,qhd->khd', probs_b, grad_tile)
        return ((grad_k, grad_v), grad_q.reshape(TQ, C))
    zeros_kv = jnp.zeros((KEYS, H, HD), jnp.float32)
    (grad_k, grad_v), grad_q = lax.scan(tile_step, (zeros_kv, zeros_kv), jnp.arange(TILES, dtype=jnp.int32))
    grad_queries = grad_q.reshape(QUERIES, C).astype(jnp.bfloat16)
    grad_keys = grad_k.reshape(KEYS, C).astype(jnp.bfloat16)
    grad_values = grad_v.reshape(KEYS, C).astype(jnp.bfloat16)
    return (grad_queries, grad_keys, grad_values)
```

```python
import functools
import math

import jax
import jax.numpy as jnp
from jax import lax
from jax.experimental import pallas as pl
from jax.experimental.pallas import tpu as pltpu
from jax.sharding import PartitionSpec as P

H = 8
LANES = 128
FAR = -1e30
BF16 = jnp.bfloat16
F32 = jnp.float32


def dot(a, b, dims):
    return lax.dot_general(a, b, (dims, ((), ())), preferred_element_type=F32)


NN = ((1,), (0,))
NT = ((1,), (1,))


def step_orders(tiles):
    bits = []
    bit = tiles // 4
    while bit >= 1:
        bits.append(bit)
        bit //= 2
    return (tuple(bits), tuple(bits[-1:] + bits[:-1]))


def slot_masks(order):
    masks = [0]
    for bit in order:
        masks = masks + [mask ^ bit for mask in masks]
    return masks


def tile_rows_mask(rows, step, index):
    return lax.broadcasted_iota(jnp.int32, rows, 0) // step == index


def build_bias(where_ref, table_ref, bias_ref, masks, shard_rows, block_keys):
    tile, cam = where_ref[0], where_ref[1]
    per_shard = shard_rows // block_keys
    lanes = table_ref.shape[1]
    table = table_ref[...]
    lane = lax.broadcasted_iota(jnp.int32, (shard_rows, lanes), 1)
    row = lax.broadcasted_iota(jnp.int32, (shard_rows, lanes), 0)
    place = lax.broadcasted_iota(jnp.int32, (shard_rows, LANES), 0) % block_keys
    column = lax.broadcasted_iota(jnp.int32, (shard_rows, LANES), 1)
    for slot in range(len(masks[0])):
        mask = jnp.where(cam % 2 == 0, masks[0][slot], masks[1][slot])
        block = (tile ^ mask) * per_shard + row // block_keys
        picked = dot((lane == block).astype(F32).astype(BF16), table, NT)
        count = picked[:, LANES - 1 : LANES]
        allowed = (picked > 0.5) & (place.astype(F32) < count)
        bias = jnp.where(allowed | (column == LANES - 1), 0.0, FAR)
        bias_ref[slot * shard_rows : (slot + 1) * shard_rows, :] = bias.astype(BF16)


def head_terms(i, half, part, span, tile_rows, keys, values, bias, query_t_ref, grad_t_ref):
    columns = slice(part * span, (part + 1) * span)
    rows = slice(half * LANES, (half + 1) * LANES)
    inside = tile_rows_mask((LANES, span), 32, i)
    zero = jnp.zeros((LANES, span), BF16)
    query_t = jnp.where(inside, query_t_ref[rows, columns], zero)
    grad_t = jnp.where(inside, grad_t_ref[rows, columns], zero)
    tile_of = (lax.broadcasted_iota(jnp.int32, (LANES, span), 1) + part * span) // tile_rows
    hot = (lax.broadcasted_iota(jnp.int32, (LANES, span), 0) == tile_of).astype(F32).astype(BF16)
    right = jnp.concatenate((query_t, hot), axis=0)
    left = jnp.concatenate((keys[half], bias), axis=1)
    return dot(left, right, NN), dot(values[half], grad_t, NN)


def chunk_of(ref, width):
    keys = [ref[:, k * LANES : (k + 1) * LANES] for k in range(width // LANES)]
    values = [ref[:, width + k * LANES : width + (k + 1) * LANES] for k in range(width // LANES)]
    return keys, values


def stats_loop(ref, bias, query_t_ref, grad_t_ref, before_ref, stats_ref, width, span, tile_rows, factor):
    keys, values = chunk_of(ref, width)
    queries = query_t_ref.shape[1]
    per_half = H // (width // LANES)

    def body(i, carry):
        for half in range(width // LANES):
            for part in range(queries // span):
                scores, dprobs = head_terms(
                    i, half, part, span, tile_rows, keys, values, bias, query_t_ref, grad_t_ref
                )
                columns = slice(part * span, (part + 1) * span)
                head = half * per_half + i
                top = jnp.max(scores, axis=0, keepdims=True)
                if before_ref is not None:
                    old_top = before_ref[pl.ds(head, 1), columns]
                    top = jnp.maximum(top, old_top)
                weights = jnp.exp2((scores - top) * factor)
                total = jnp.sum(weights, axis=0, keepdims=True)
                product = jnp.sum(weights * dprobs, axis=0, keepdims=True)
                if before_ref is not None:
                    shrink = jnp.exp2((old_top - top) * factor)
                    total = total + shrink * before_ref[pl.ds(H + head, 1), columns]
                    product = product + shrink * before_ref[pl.ds(2 * H + head, 1), columns]
                stats_ref[pl.ds(head, 1), columns] = top
                stats_ref[pl.ds(H + head, 1), columns] = total
                stats_ref[pl.ds(2 * H + head, 1), columns] = product
        return carry

    lax.fori_loop(0, per_half, body, 0)


def first_kernel(cams, masks, shard_rows, block_keys, span, tile_rows, factor, where_ref, query_ref, grad_ref, *refs):
    pieces, (chunk_ref, table_ref), outs = refs[:cams], refs[cams : cams + 2], refs[cams + 2 :]
    stats_ref, query_full_ref, grad_full_ref, query_t_ref, grad_t_ref, bias_ref, far_ref = outs
    rows, width = query_ref.shape
    build_bias(where_ref, table_ref, bias_ref, masks, shard_rows, block_keys)
    piece_rows = 2 * rows // cams
    for shift in range(cams):
        piece = lax.rem(where_ref[1] + cams - shift, cams)
        start = pl.multiple_of(piece * piece_rows, 16)
        far_ref[pl.ds(start, piece_rows), :] = pieces[shift][:piece_rows, :]
    query_full_ref[:rows, :] = query_ref[...]
    query_full_ref[rows:, :] = far_ref[:rows, :]
    grad_full_ref[:rows, :] = grad_ref[...]
    grad_full_ref[rows:, :] = far_ref[rows:, :]
    query_t_ref[...] = query_full_ref[...].T
    grad_t_ref[...] = grad_full_ref[...].T
    bias = bias_ref[: chunk_ref.shape[0], :]
    stats_loop(chunk_ref, bias, query_t_ref, grad_t_ref, None, stats_ref, width, span, tile_rows, factor)


def second_kernel(span, tile_rows, factor, chunk_ref, bias_ref, query_t_ref, grad_t_ref, before_ref, stats_ref):
    width = query_t_ref.shape[0]
    bias = bias_ref[chunk_ref.shape[0] :, :]
    stats_loop(chunk_ref, bias, query_t_ref, grad_t_ref, before_ref, stats_ref, width, span, tile_rows, factor)


def gradients(which, span, tile_rows, factor, scale, chunk_ref, bias_ref, query_full_ref, grad_full_ref, query_t_ref,
              grad_t_ref, ends_ref, out_ref, query_sum_ref, probs_ref, dscores_ref, query_m_ref, grad_m_ref):
    width = query_t_ref.shape[0]
    queries = query_t_ref.shape[1]
    count = chunk_ref.shape[0]
    halves = width // LANES
    per_half = H // halves
    head_dim = width // H
    keys, values = chunk_of(chunk_ref, width)
    keys_t = chunk_ref[:, :width].T
    bias = bias_ref[which * count : (which + 1) * count, :]

    for i in range(per_half):
        inside = lax.broadcasted_iota(jnp.int32, (queries, LANES), 1) // head_dim == i
        zero = jnp.zeros((queries, LANES), BF16)
        for half in range(halves):
            columns = slice(half * LANES, (half + 1) * LANES)
            rows = slice(i * queries, (i + 1) * queries)
            query_m_ref[half, rows, :] = jnp.where(inside, query_full_ref[:, columns], zero)
            grad_m_ref[half, rows, :] = jnp.where(inside, grad_full_ref[:, columns], zero)

    for half in range(halves):
        for i in range(per_half):
            head = half * per_half + i
            key_t = keys_t[head * head_dim : (head + 1) * head_dim, :]
            for part in range(queries // span):
                scores, dprobs = head_terms(
                    i, half, part, span, tile_rows, keys, values, bias, query_t_ref, grad_t_ref
                )
                columns = slice(part * span, (part + 1) * span)
                probs = jnp.exp2(scores * factor - ends_ref[head : head + 1, columns])
                dscores = (probs * (dprobs - ends_ref[H + head : H + head + 1, columns])).astype(BF16)
                place = slice(i * queries + part * span, i * queries + (part + 1) * span)
                probs_ref[:, place] = probs.astype(BF16)
                dscores_ref[:, place] = dscores
                piece = dot(key_t, dscores, NN)
                rows = slice(head * head_dim, (head + 1) * head_dim)
                if which == 1:
                    query_sum_ref[rows, columns] = piece
                else:
                    query_sum_ref[rows, columns] += piece
        grad_k = dot(dscores_ref[...], query_m_ref[half], NN) * scale
        grad_v = dot(probs_ref[...], grad_m_ref[half], NN)
        out_ref[:, half * LANES : (half + 1) * LANES] = grad_k.astype(out_ref.dtype)
        out_ref[:, width + half * LANES : width + (half + 1) * LANES] = grad_v.astype(out_ref.dtype)


def third_kernel(span, tile_rows, factor, scale, near_ref, across_ref, chunk_ref, bias_ref, query_full_ref, grad_full_ref,
                 query_t_ref, grad_t_ref, out_ref, query_sum_ref, ends_ref, *scratch):
    rows = near_ref.shape[1] // 2
    turned = jnp.concatenate((across_ref[:, rows:], across_ref[:, :rows]), axis=1)
    near_top, across_top = near_ref[:H, :], turned[:H, :]
    top = jnp.maximum(near_top, across_top)
    near, across = jnp.exp2((near_top - top) * factor), jnp.exp2((across_top - top) * factor)
    total = near * near_ref[H : 2 * H, :] + across * turned[H : 2 * H, :]
    product = near * near_ref[2 * H :, :] + across * turned[2 * H :, :]
    ends_ref[:H, :] = top * factor + jnp.log2(total)
    ends_ref[H:, :] = product / total
    gradients(1, span, tile_rows, factor, scale, chunk_ref, bias_ref, query_full_ref, grad_full_ref, query_t_ref,
              grad_t_ref, ends_ref, out_ref, query_sum_ref, *scratch)


def fourth_kernel(span, tile_rows, factor, scale, ends_ref, before_ref, chunk_ref, bias_ref, query_full_ref, grad_full_ref,
                  query_t_ref, grad_t_ref, out_ref, own_ref, far_ref, query_sum_ref, *scratch):
    query_sum_ref[...] = before_ref[...]
    gradients(0, span, tile_rows, factor, scale, chunk_ref, bias_ref, query_full_ref, grad_full_ref, query_t_ref,
              grad_t_ref, ends_ref, out_ref, query_sum_ref, *scratch)
    rows = own_ref.shape[0]
    sums = query_sum_ref[...].T * scale
    own_ref[...] = sums[:rows, :]
    far_ref[...] = sums[rows:, :].astype(BF16)


def run(kernel, outs, args, scratch=(), smem=0, flops=0):
    size = lambda a: math.prod(a.shape) * a.dtype.itemsize
    moved = sum(size(a) for a in args) + sum(size(a) for a in outs)
    vmem = pl.BlockSpec(memory_space=pltpu.VMEM)
    return pl.pallas_call(
        kernel,
        out_shape=tuple(outs),
        in_specs=[pl.BlockSpec(memory_space=pltpu.SMEM)] * smem + [vmem] * (len(args) - smem),
        out_specs=tuple([vmem] * len(outs)),
        scratch_shapes=list(scratch),
        cost_estimate=pl.CostEstimate(flops=flops, bytes_accessed=moved, transcendentals=flops // 64),
        compiler_params=pltpu.CompilerParams(vmem_limit_bytes=40 * 1024 * 1024),
    )(*args)


def combine(parts, factor):
    top = functools.reduce(jnp.maximum, [part[:H] for part in parts])
    shrink = [jnp.exp2((part[:H] - top) * factor) for part in parts]
    total = sum(s * part[H : 2 * H] for s, part in zip(shrink, parts))
    product = sum(s * part[2 * H :] for s, part in zip(shrink, parts))
    return jnp.concatenate((top, total, product), axis=0)


def shards(queries, keys, values, grad_out, visible, counts):
    rows, width = queries.shape
    shard_rows = keys.shape[0]
    head_dim = width // H
    scale = 1.0 / math.sqrt(head_dim)
    factor = scale * math.log2(math.e)
    tiles, cams = lax.axis_size("tile"), lax.axis_size("cam")
    tile, cam = lax.axis_index("tile"), lax.axis_index("cam")
    blocks = counts.shape[0]
    block_keys = shard_rows * tiles // blocks
    own_tiles = visible.shape[0]
    tile_rows = rows // own_tiles
    orders = step_orders(tiles)
    masks = [slot_masks(order) for order in orders]
    span = 256

    def across(x, hop):
        pairs = [(c * tiles + t, c * tiles + (t ^ hop(c))) for c in range(cams) for t in range(tiles)]
        return lax.ppermute(x, ("cam", "tile"), pairs)

    def step(x, k):
        return across(x, lambda c: orders[c % 2][k])

    def swap_half(x):
        return across(x, lambda c: tiles // 2)

    def turn(x, shift):
        return lax.ppermute(x, "cam", [(c, (c + shift) % cams) for c in range(cams)])

    steps = len(orders[0])
    joined = jnp.concatenate((keys, values), axis=1)
    both = jnp.concatenate((queries, grad_out), axis=0)
    piece_rows = 2 * rows // cams
    mine = lax.dynamic_slice_in_dim(both, cam * piece_rows, piece_rows, 0)
    note = jnp.pad(visible.astype(BF16), ((0, 16 - own_tiles), (0, width - blocks)))
    received = swap_half(jnp.concatenate((mine, note), axis=0))
    held = joined
    for k in range(steps - 1):
        held = jnp.concatenate((held, step(held, k)), axis=0)
    pieces = [received] + [turn(received, shift) for shift in range(1, cams)]
    last = step(held, steps - 1)

    lanes = -(-blocks // LANES) * LANES
    own_seen = jnp.pad(visible.astype(BF16), ((0, 0), (0, lanes - blocks)))
    far_seen = jnp.pad(received[piece_rows : piece_rows + own_tiles, :blocks], ((0, 0), (0, lanes - blocks)))
    limit = jnp.pad(counts.astype(BF16)[None, :], ((0, 0), (0, lanes - blocks)))
    table = jnp.concatenate(
        (own_seen, far_seen, jnp.zeros((LANES - 1 - 2 * own_tiles, lanes), BF16), limit), axis=0
    )
    where = jnp.stack((tile, cam)).astype(jnp.int32)

    shape = jax.ShapeDtypeStruct
    all_rows = 2 * rows
    chunk = held.shape[0]
    work = 2 * all_rows * chunk * width
    stats, query_full, grad_full, query_t, grad_t, bias = run(
        functools.partial(first_kernel, cams, masks, shard_rows, block_keys, span, tile_rows, factor),
        (
            shape((3 * H, all_rows), F32),
            shape((all_rows, width), BF16),
            shape((all_rows, width), BF16),
            shape((width, all_rows), BF16),
            shape((width, all_rows), BF16),
            shape((2 * chunk, LANES), BF16),
        ),
        (where, queries, grad_out, *pieces, held, table),
        scratch=(pltpu.VMEM((2 * rows, width), BF16),),
        smem=1,
        flops=8 * work,
    )
    (stats,) = run(
        functools.partial(second_kernel, span, tile_rows, factor),
        (shape((3 * H, all_rows), F32),),
        (last, bias, query_t, grad_t, stats),
        flops=8 * work,
    )
    near = combine([stats] + [turn(stats, shift) for shift in range(1, cams)], factor)
    opposite = swap_half(near)

    halves = width // LANES
    scratch = (
        pltpu.VMEM((chunk, H // halves * all_rows), BF16),
        pltpu.VMEM((chunk, H // halves * all_rows), BF16),
        pltpu.VMEM((halves, H // halves * all_rows, LANES), BF16),
        pltpu.VMEM((halves, H // halves * all_rows, LANES), BF16),
    )
    common = (bias, query_full, grad_full, query_t, grad_t)
    sent, query_sum, ends = run(
        functools.partial(third_kernel, span, tile_rows, factor, scale),
        (shape((chunk, 2 * width), BF16), shape((width, all_rows), F32), shape((2 * H, all_rows), F32)),
        (near, opposite, last, *common),
        scratch=scratch,
        flops=20 * work,
    )
    got = step(sent, steps - 1)
    kept, query_own, query_far = run(
        functools.partial(fourth_kernel, span, tile_rows, factor, scale),
        (shape((chunk, 2 * width), F32), shape((rows, width), F32), shape((rows, width), BF16)),
        (ends, query_sum, held, *common),
        scratch=(pltpu.VMEM((width, all_rows), F32), *scratch),
        flops=20 * work,
    )
    query_got = swap_half(query_far)
    size = chunk
    for k in range(steps - 2, -1, -1):
        size //= 2
        out = (kept[size:] + got[size:].astype(F32)).astype(BF16)
        kept = kept[:size] + got[:size].astype(F32)
        got = step(out, k)
    owned = (kept + got.astype(F32)).astype(BF16)
    query_part = query_own + query_got.astype(F32)
    to_turn = query_part.astype(BF16)
    for shift in range(1, cams):
        query_part = query_part + turn(to_turn, shift).astype(F32)
    return (query_part.astype(BF16), owned[:, :width], owned[:, width:])


def solution(mesh):
    in_specs = (
        P("tile", None),
        P(("cam", "tile"), None),
        P(("cam", "tile"), None),
        P("tile", None),
        P("tile", "cam"),
        P("cam"),
    )
    out_specs = (P("tile", None), P(("cam", "tile"), None), P(("cam", "tile"), None))
    return jax.shard_map(shards, mesh=mesh, in_specs=in_specs, out_specs=out_specs, check_vma=False)
```

```python
import functools
import math

import jax
import jax.numpy as jnp
from jax import lax
from jax.experimental import pallas as pl
from jax.experimental.pallas import tpu as pltpu
from jax.sharding import PartitionSpec as P


H = 8
LANES = 128
FAR = -1e30
BF16 = jnp.bfloat16
F32 = jnp.float32


def dot(a, b, dims):
    return lax.dot_general(a, b, (dims, ((), ())), preferred_element_type=F32)


NN = ((1,), (0,))
NT = ((1,), (1,))


def step_orders(tiles):
    bits = []
    bit = tiles // 4
    while bit >= 1:
        bits.append(bit)
        bit //= 2
    return (tuple(bits), tuple(bits[-1:] + bits[:-1]))


def slot_masks(order):
    masks = [0]
    for bit in order:
        masks = masks + [mask ^ bit for mask in masks]
    return masks


def build_bias(where_ref, table_ref, bias_ref, masks, shard_rows, block_keys):
    tile, cam = where_ref[0], where_ref[1]
    per_shard = shard_rows // block_keys
    lanes = table_ref.shape[1]
    table = table_ref[...]
    lane = lax.broadcasted_iota(jnp.int32, (shard_rows, lanes), 1)
    row = lax.broadcasted_iota(jnp.int32, (shard_rows, lanes), 0)
    place = lax.broadcasted_iota(jnp.int32, (shard_rows, LANES), 0) % block_keys
    column = lax.broadcasted_iota(jnp.int32, (shard_rows, LANES), 1)
    for slot in range(len(masks[0])):
        mask = jnp.where(cam % 2 == 0, masks[0][slot], masks[1][slot])
        block = (tile ^ mask) * per_shard + row // block_keys
        picked = dot((lane == block).astype(F32).astype(BF16), table, NT)
        count = picked[:, LANES - 1 : LANES]
        allowed = (picked > 0.5) & (place.astype(F32) < count)
        bias = jnp.where(allowed | (column == LANES - 1), 0.0, FAR)
        bias_ref[slot * shard_rows : (slot + 1) * shard_rows, :] = bias.astype(BF16)


def head_terms(head, span, first, tile_rows, keys, values, bias, query_t, grad_t):
    size = query_t.shape[0]
    half, inside = head * size // LANES, head * size % LANES

    def alone(rows):
        parts = [jnp.zeros((inside, span), BF16)] if inside else []
        parts.append(rows)
        if inside + size < LANES:
            parts.append(jnp.zeros((LANES - inside - size, span), BF16))
        return jnp.concatenate(parts, axis=0)

    tile_of = (lax.broadcasted_iota(jnp.int32, (LANES, span), 1) + first) // tile_rows
    hot = (lax.broadcasted_iota(jnp.int32, (LANES, span), 0) == tile_of).astype(F32).astype(BF16)
    right = jnp.concatenate((alone(query_t), hot), axis=0)
    left = jnp.concatenate((keys[half], bias), axis=1)
    return dot(left, right, NN), dot(values[half], alone(grad_t), NN)


def chunk_of(ref, width):
    keys = [ref[:, k * LANES : (k + 1) * LANES] for k in range(width // LANES)]
    values = [ref[:, width + k * LANES : width + (k + 1) * LANES] for k in range(width // LANES)]
    return keys, values


def stats_of(ref, bias, query_t_ref, grad_t_ref, before_ref, stats_ref, span, tile_rows, factor):
    width, queries = query_t_ref.shape
    keys, values = chunk_of(ref, width)
    for head in range(H):
        rows = slice(head * width // H, (head + 1) * width // H)
        for first in range(0, queries, span):
            columns = slice(first, first + span)
            scores, dprobs = head_terms(
                head, span, first, tile_rows, keys, values, bias, query_t_ref[rows, columns], grad_t_ref[rows, columns]
            )
            top = jnp.max(scores, axis=0, keepdims=True)
            if before_ref is not None:
                old_top = before_ref[head : head + 1, columns]
                top = jnp.maximum(top, old_top)
            weights = jnp.exp2((scores - top) * factor)
            total = jnp.sum(weights, axis=0, keepdims=True)
            product = jnp.sum(weights * dprobs, axis=0, keepdims=True)
            if before_ref is not None:
                shrink = jnp.exp2((old_top - top) * factor)
                total = total + shrink * before_ref[H + head : H + head + 1, columns]
                product = product + shrink * before_ref[2 * H + head : 2 * H + head + 1, columns]
            stats_ref[head : head + 1, columns] = top
            stats_ref[H + head : H + head + 1, columns] = total
            stats_ref[2 * H + head : 2 * H + head + 1, columns] = product


def first_kernel(cams, masks, shard_rows, block_keys, span, tile_rows, factor, where_ref, query_ref, grad_ref, *refs):
    pieces, (chunk_ref, table_ref), outs = refs[:cams], refs[cams : cams + 2], refs[cams + 2 :]
    stats_ref, query_t_ref, grad_t_ref, bias_ref, far_ref = outs
    rows, _ = query_ref.shape
    build_bias(where_ref, table_ref, bias_ref, masks, shard_rows, block_keys)
    piece_rows = 2 * rows // cams
    for shift in range(cams):
        piece = lax.rem(where_ref[1] + cams - shift, cams)
        start = pl.multiple_of(piece * piece_rows, 16)
        far_ref[pl.ds(start, piece_rows), :] = pieces[shift][:piece_rows, :]
    query_t_ref[:, :rows] = query_ref[...].T
    query_t_ref[:, rows:] = far_ref[:rows, :].T
    grad_t_ref[:, :rows] = grad_ref[...].T
    grad_t_ref[:, rows:] = far_ref[rows:, :].T
    bias = bias_ref[: chunk_ref.shape[0], :]
    stats_of(chunk_ref, bias, query_t_ref, grad_t_ref, None, stats_ref, span, tile_rows, factor)


def second_kernel(span, tile_rows, factor, chunk_ref, bias_ref, query_t_ref, grad_t_ref, before_ref, stats_ref):
    bias = bias_ref[chunk_ref.shape[0] :, :]
    stats_of(chunk_ref, bias, query_t_ref, grad_t_ref, before_ref, stats_ref, span, tile_rows, factor)


def gradients(which, span, tile_rows, factor, scale, chunk_ref, bias_ref, query_t_ref, grad_t_ref, ends_ref, out_ref,
              query_sum_ref, before_ref, sums_ref):
    width, queries = query_t_ref.shape
    count = chunk_ref.shape[0]
    keys, values = chunk_of(chunk_ref, width)
    keys_t = chunk_ref[:, :width].T
    bias = bias_ref[which * count : (which + 1) * count, :]
    blocks = [(head, first) for head in range(H) for first in range(0, queries, span)]

    def rows_of(head):
        return slice(head * width // H, (head + 1) * width // H)

    def terms(head, first):
        rows, columns = rows_of(head), slice(first, first + span)
        return head_terms(
            head, span, first, tile_rows, keys, values, bias, query_t_ref[rows, columns], grad_t_ref[rows, columns]
        )

    def rounded(head, first, scores, dprobs):
        columns = slice(first, first + span)
        probs = jnp.exp2(scores * factor - ends_ref[head : head + 1, columns])
        dscores = (probs * (dprobs - ends_ref[H + head : H + head + 1, columns])).astype(BF16)
        return probs.astype(BF16), dscores

    def products(head, first, probs, dscores, sums):
        rows, columns = rows_of(head), slice(first, first + span)
        key_part = dot(query_t_ref[rows, columns], dscores, NT)
        value_part = dot(grad_t_ref[rows, columns], probs, NT)
        piece = dot(keys_t[rows, :], dscores, NN)
        if before_ref is not None:
            piece += before_ref[rows, columns]
        query_sum_ref[rows, columns] = piece
        sums = (key_part, value_part) if first == 0 else (sums[0] + key_part, sums[1] + value_part)
        if first + span == queries:
            sums_ref[rows, :] = sums[0] * scale
            sums_ref[width + rows.start : width + rows.stop, :] = sums[1]
        return sums

    ahead, lag = 1, 2
    raw, ready, sums = {}, {}, None
    for n in range(len(blocks) + ahead + lag):
        if n < len(blocks):
            raw[n] = terms(*blocks[n])
        if 0 <= n - ahead < len(blocks):
            ready[n - ahead] = rounded(*blocks[n - ahead], *raw.pop(n - ahead))
        if 0 <= n - ahead - lag:
            sums = products(*blocks[n - ahead - lag], *ready.pop(n - ahead - lag), sums)
    out_ref[...] = sums_ref[...].T.astype(out_ref.dtype)


def third_kernel(span, tile_rows, factor, scale, near_ref, across_ref, chunk_ref, bias_ref, query_t_ref, grad_t_ref,
                 out_ref, query_sum_ref, ends_ref, sums_ref):
    rows = near_ref.shape[1] // 2
    turned = jnp.concatenate((across_ref[:, rows:], across_ref[:, :rows]), axis=1)
    near_top, across_top = near_ref[:H, :], turned[:H, :]
    top = jnp.maximum(near_top, across_top)
    near, across = jnp.exp2((near_top - top) * factor), jnp.exp2((across_top - top) * factor)
    total = near * near_ref[H : 2 * H, :] + across * turned[H : 2 * H, :]
    product = near * near_ref[2 * H :, :] + across * turned[2 * H :, :]
    ends_ref[:H, :] = top * factor + jnp.log2(total)
    ends_ref[H:, :] = product / total
    gradients(1, span, tile_rows, factor, scale, chunk_ref, bias_ref, query_t_ref, grad_t_ref, ends_ref, out_ref,
              query_sum_ref, None, sums_ref)


def fourth_kernel(span, tile_rows, factor, scale, ends_ref, before_ref, chunk_ref, bias_ref, query_t_ref, grad_t_ref,
                  out_ref, own_ref, far_ref, query_sum_ref, sums_ref):
    gradients(0, span, tile_rows, factor, scale, chunk_ref, bias_ref, query_t_ref, grad_t_ref, ends_ref, out_ref,
              query_sum_ref, before_ref, sums_ref)
    rows = own_ref.shape[0]
    sums = query_sum_ref[...].T * scale
    own_ref[...] = sums[:rows, :]
    far_ref[...] = sums[rows:, :].astype(BF16)


def run(kernel, outs, args, scratch=(), smem=0, flops=0):
    size = lambda a: math.prod(a.shape) * a.dtype.itemsize
    moved = sum(size(a) for a in args) + sum(size(a) for a in outs)
    vmem = pl.BlockSpec(memory_space=pltpu.VMEM)
    return pl.pallas_call(
        kernel,
        out_shape=tuple(outs),
        in_specs=[pl.BlockSpec(memory_space=pltpu.SMEM)] * smem + [vmem] * (len(args) - smem),
        out_specs=tuple([vmem] * len(outs)),
        scratch_shapes=list(scratch),
        cost_estimate=pl.CostEstimate(flops=flops, bytes_accessed=moved, transcendentals=flops // 64),
        compiler_params=pltpu.CompilerParams(vmem_limit_bytes=40 * 1024 * 1024),
    )(*args)


def combine(parts, factor):
    top = functools.reduce(jnp.maximum, [part[:H] for part in parts])
    shrink = [jnp.exp2((part[:H] - top) * factor) for part in parts]
    total = sum(s * part[H : 2 * H] for s, part in zip(shrink, parts))
    product = sum(s * part[2 * H :] for s, part in zip(shrink, parts))
    return jnp.concatenate((top, total, product), axis=0)


def shards(queries, keys, values, grad_out, visible, counts):
    rows, width = queries.shape
    shard_rows = keys.shape[0]
    head_dim = width // H
    scale = 1.0 / math.sqrt(head_dim)
    factor = scale * math.log2(math.e)
    tiles, cams = lax.axis_size("tile"), lax.axis_size("cam")
    tile, cam = lax.axis_index("tile"), lax.axis_index("cam")
    blocks = counts.shape[0]
    block_keys = shard_rows * tiles // blocks
    own_tiles = visible.shape[0]
    tile_rows = rows // own_tiles
    orders = step_orders(tiles)
    masks = [slot_masks(order) for order in orders]
    span = 256

    def across(x, hop):
        pairs = [(c * tiles + t, c * tiles + (t ^ hop(c))) for c in range(cams) for t in range(tiles)]
        return lax.ppermute(x, ("cam", "tile"), pairs)

    def step(x, k):
        return across(x, lambda c: orders[c % 2][k])

    def swap_half(x):
        return across(x, lambda c: tiles // 2)

    def turn(x, shift):
        return lax.ppermute(x, "cam", [(c, (c + shift) % cams) for c in range(cams)])

    steps = len(orders[0])
    joined = jnp.concatenate((keys, values), axis=1)
    both = jnp.concatenate((queries, grad_out), axis=0)
    piece_rows = 2 * rows // cams
    mine = lax.dynamic_slice_in_dim(both, cam * piece_rows, piece_rows, 0)
    note = jnp.pad(visible.astype(BF16), ((0, 16 - own_tiles), (0, width - blocks)))
    received = swap_half(jnp.concatenate((mine, note), axis=0))
    held = joined
    for k in range(steps - 1):
        held = jnp.concatenate((held, step(held, k)), axis=0)
    pieces = [received] + [turn(received, shift) for shift in range(1, cams)]
    last = step(held, steps - 1)

    lanes = -(-blocks // LANES) * LANES
    own_seen = jnp.pad(visible.astype(BF16), ((0, 0), (0, lanes - blocks)))
    far_seen = jnp.pad(received[piece_rows : piece_rows + own_tiles, :blocks], ((0, 0), (0, lanes - blocks)))
    limit = jnp.pad(counts.astype(BF16)[None, :], ((0, 0), (0, lanes - blocks)))
    table = jnp.concatenate(
        (own_seen, far_seen, jnp.zeros((LANES - 1 - 2 * own_tiles, lanes), BF16), limit), axis=0
    )
    where = jnp.stack((tile, cam)).astype(jnp.int32)

    shape = jax.ShapeDtypeStruct
    all_rows = 2 * rows
    chunk = held.shape[0]
    work = 2 * all_rows * chunk * width
    stats, query_t, grad_t, bias = run(
        functools.partial(first_kernel, cams, masks, shard_rows, block_keys, span, tile_rows, factor),
        (
            shape((3 * H, all_rows), F32),
            shape((width, all_rows), BF16),
            shape((width, all_rows), BF16),
            shape((2 * chunk, LANES), BF16),
        ),
        (where, queries, grad_out, *pieces, held, table),
        scratch=(pltpu.VMEM((2 * rows, width), BF16),),
        smem=1,
        flops=8 * work,
    )
    (stats,) = run(
        functools.partial(second_kernel, span, tile_rows, factor),
        (shape((3 * H, all_rows), F32),),
        (last, bias, query_t, grad_t, stats),
        flops=8 * work,
    )
    near = combine([stats] + [turn(stats, shift) for shift in range(1, cams)], factor)
    opposite = swap_half(near)

    scratch = (pltpu.VMEM((2 * width, chunk), F32),)
    common = (bias, query_t, grad_t)
    sent, query_sum, ends = run(
        functools.partial(third_kernel, span, tile_rows, factor, scale),
        (shape((chunk, 2 * width), BF16), shape((width, all_rows), F32), shape((2 * H, all_rows), F32)),
        (near, opposite, last, *common),
        scratch=scratch,
        flops=20 * work,
    )
    got = step(sent, steps - 1)
    kept, query_own, query_far = run(
        functools.partial(fourth_kernel, span, tile_rows, factor, scale),
        (shape((chunk, 2 * width), F32), shape((rows, width), F32), shape((rows, width), BF16)),
        (ends, query_sum, held, *common),
        scratch=(pltpu.VMEM((width, all_rows), F32), *scratch),
        flops=20 * work,
    )
    query_got = swap_half(query_far)
    size = chunk
    for k in range(steps - 2, -1, -1):
        size //= 2
        out = (kept[size:] + got[size:].astype(F32)).astype(BF16)
        kept = kept[:size] + got[:size].astype(F32)
        got = step(out, k)
    owned = (kept + got.astype(F32)).astype(BF16)
    query_part = query_own + query_got.astype(F32)
    to_turn = query_part.astype(BF16)
    for shift in range(1, cams):
        query_part = query_part + turn(to_turn, shift).astype(F32)
    return (query_part.astype(BF16), owned[:, :width], owned[:, width:])


def solution(mesh):
    in_specs = (
        P("tile", None),
        P(("cam", "tile"), None),
        P(("cam", "tile"), None),
        P("tile", None),
        P("tile", "cam"),
        P("cam"),
    )
    out_specs = (P("tile", None), P(("cam", "tile"), None), P(("cam", "tile"), None))

    return jax.shard_map(shards, mesh=mesh, in_specs=in_specs, out_specs=out_specs, check_vma=False)
```

```python
import functools
import math

import jax
import jax.numpy as jnp
from jax import lax
from jax.experimental import pallas as pl
from jax.experimental.pallas import tpu as pltpu
from jax.sharding import PartitionSpec as P


H = 8
LANES = 128
FAR = -1e30
BF16 = jnp.bfloat16
F32 = jnp.float32


def dot(a, b, dims):
    return lax.dot_general(a, b, (dims, ((), ())), preferred_element_type=F32)


NN = ((1,), (0,))
NT = ((1,), (1,))


def step_orders(tiles):
    bits = []
    bit = 1
    while bit < tiles // 2:
        bits.append(bit)
        bit *= 2
    return (tuple(bits[::-1]), tuple(bits[:1:-1] + bits[:2]))


def slot_masks(order):
    masks = [0]
    for bit in order:
        masks = masks + [mask ^ bit for mask in masks]
    return masks


def start_kernel(cams, where_ref, key_ref, value_ref, query_ref, grad_ref, seen_ref, limit_ref, pair_ref, query_out,
                 grad_out, message_ref, table_ref, seen_vmem, limit_vmem, sems):
    rows, width = query_ref.shape
    own_tiles, blocks = seen_ref.shape
    moves = (
        (query_ref, query_out),
        (grad_ref, grad_out),
        (seen_ref, seen_vmem),
        (limit_ref, limit_vmem),
        (key_ref, pair_ref.at[:, :width]),
        (value_ref, pair_ref.at[:, width:]),
    )
    copies = [pltpu.make_async_copy(source, target, sems.at[k]) for k, (source, target) in enumerate(moves)]
    for copy in copies:
        copy.start()
    piece_rows = 2 * rows // cams
    message_ref[piece_rows:, :] = jnp.zeros((16, width), BF16)
    table_ref[...] = jnp.zeros(table_ref.shape, BF16)
    for copy in copies:
        copy.wait()
    for piece in range(cams):

        @pl.when(where_ref[1] == piece)
        def _(first=piece * piece_rows):
            source, at = (query_out, first) if first < rows else (grad_out, first - rows)
            message_ref[:piece_rows, :] = source[at : at + piece_rows, :]

    seen = seen_vmem[...].astype(F32).astype(BF16)
    message_ref[piece_rows : piece_rows + own_tiles, :blocks] = seen
    table_ref[:own_tiles, :blocks] = seen
    table_ref[LANES - 1 : LANES, :blocks] = limit_vmem[...].astype(F32).astype(BF16)


def build_bias(where_ref, table_ref, bias_ref, masks, shard_rows, block_keys):
    tile, cam = where_ref[0], where_ref[1]
    per_shard = shard_rows // block_keys
    lanes = table_ref.shape[1]
    table = table_ref[...]
    lane = lax.broadcasted_iota(jnp.int32, (shard_rows, lanes), 1)
    row = lax.broadcasted_iota(jnp.int32, (shard_rows, lanes), 0)
    place = lax.broadcasted_iota(jnp.int32, (shard_rows, LANES), 0) % block_keys
    column = lax.broadcasted_iota(jnp.int32, (shard_rows, LANES), 1)
    for slot in range(len(masks[0])):
        mask = jnp.where(cam % 2 == 0, masks[0][slot], masks[1][slot])
        block = (tile ^ mask) * per_shard + row // block_keys
        picked = dot((lane == block).astype(F32).astype(BF16), table, NT)
        count = picked[:, LANES - 1 : LANES]
        allowed = (picked > 0.5) & (place.astype(F32) < count)
        bias = jnp.where(allowed | (column == LANES - 1), 0.0, FAR)
        bias_ref[slot * shard_rows : (slot + 1) * shard_rows, :] = bias.astype(BF16)


def head_terms(head, span, first, tile_rows, keys, values, bias, query_t, grad_t):
    size = query_t.shape[0]
    half, inside = head * size // LANES, head * size % LANES

    def alone(rows):
        parts = [jnp.zeros((inside, span), BF16)] if inside else []
        parts.append(rows)
        if inside + size < LANES:
            parts.append(jnp.zeros((LANES - inside - size, span), BF16))
        return jnp.concatenate(parts, axis=0)

    tile_of = (lax.broadcasted_iota(jnp.int32, (LANES, span), 1) + first) // tile_rows
    hot = (lax.broadcasted_iota(jnp.int32, (LANES, span), 0) == tile_of).astype(F32).astype(BF16)
    right = jnp.concatenate((alone(query_t), hot), axis=0)
    left = jnp.concatenate((keys[half], bias), axis=1)
    return dot(left, right, NN), dot(values[half], alone(grad_t), NN)


def chunk_of(ref, width):
    keys = [ref[:, k * LANES : (k + 1) * LANES] for k in range(width // LANES)]
    values = [ref[:, width + k * LANES : width + (k + 1) * LANES] for k in range(width // LANES)]
    return keys, values


def stats_of(ref, bias, query_t_ref, grad_t_ref, before_ref, stats_ref, span, tile_rows, factor):
    width, queries = query_t_ref.shape
    keys, values = chunk_of(ref, width)
    for head in range(H):
        rows = slice(head * width // H, (head + 1) * width // H)
        for first in range(0, queries, span):
            columns = slice(first, first + span)
            scores, dprobs = head_terms(
                head, span, first, tile_rows, keys, values, bias, query_t_ref[rows, columns], grad_t_ref[rows, columns]
            )
            top = jnp.max(scores, axis=0, keepdims=True)
            if before_ref is not None:
                old_top = before_ref[head : head + 1, columns]
                top = jnp.maximum(top, old_top)
            weights = jnp.exp2((scores - top) * factor)
            total = jnp.sum(weights, axis=0, keepdims=True)
            product = jnp.sum(weights * dprobs, axis=0, keepdims=True)
            if before_ref is not None:
                shrink = jnp.exp2((old_top - top) * factor)
                total = total + shrink * before_ref[H + head : H + head + 1, columns]
                product = product + shrink * before_ref[2 * H + head : 2 * H + head + 1, columns]
            stats_ref[head : head + 1, columns] = top
            stats_ref[H + head : H + head + 1, columns] = total
            stats_ref[2 * H + head : 2 * H + head + 1, columns] = product


def first_kernel(cams, blocks, masks, shard_rows, block_keys, span, tile_rows, factor, where_ref, query_ref, grad_ref, *refs):
    pieces, (chunk_ref, table_ref), outs = refs[:cams], refs[cams : cams + 2], refs[cams + 2 :]
    stats_ref, query_t_ref, grad_t_ref, bias_ref, far_ref, full_table_ref = outs
    rows, _ = query_ref.shape
    own_tiles = rows // tile_rows
    note = slice(2 * rows // cams, 2 * rows // cams + own_tiles)
    full_table_ref[...] = table_ref[...]
    full_table_ref[own_tiles : 2 * own_tiles, :blocks] = pieces[0][note, :blocks]
    build_bias(where_ref, full_table_ref, bias_ref, masks, shard_rows, block_keys)
    piece_rows = 2 * rows // cams
    for shift in range(cams):
        piece = lax.rem(where_ref[1] + cams - shift, cams)
        start = pl.multiple_of(piece * piece_rows, 16)
        far_ref[pl.ds(start, piece_rows), :] = pieces[shift][:piece_rows, :]
    query_t_ref[:, :rows] = query_ref[...].T
    query_t_ref[:, rows:] = far_ref[:rows, :].T
    grad_t_ref[:, :rows] = grad_ref[...].T
    grad_t_ref[:, rows:] = far_ref[rows:, :].T
    bias = bias_ref[: chunk_ref.shape[0], :]
    stats_of(chunk_ref, bias, query_t_ref, grad_t_ref, None, stats_ref, span, tile_rows, factor)


def second_kernel(span, tile_rows, factor, chunk_ref, bias_ref, query_t_ref, grad_t_ref, before_ref, stats_ref):
    bias = bias_ref[chunk_ref.shape[0] :, :]
    stats_of(chunk_ref, bias, query_t_ref, grad_t_ref, before_ref, stats_ref, span, tile_rows, factor)


def head_rows(head, width):
    return slice(head * width // H, (head + 1) * width // H)


def staggered(count, stages, lags):
    results = [{} for _ in stages]
    total = sum(lags)
    for n in range(count + total):
        at = n
        for k, stage in enumerate(stages):
            at -= lags[k]
            if 0 <= at < count:
                results[k][at] = stage(at) if k == 0 else stage(at, results[k - 1].pop(at))


def block_list(queries, span):
    return [(head, slice(first, first + span)) for head in range(H) for first in range(0, queries, span)]


def near_kernel(span, tile_rows, factor, near_ref, chunk_ref, bias_ref, query_t_ref, grad_t_ref, weights_ref, dprobs_ref):
    width, queries = query_t_ref.shape
    keys, values = chunk_of(chunk_ref, width)
    bias = bias_ref[chunk_ref.shape[0] :, :]
    blocks = block_list(queries, span)

    def terms(n):
        head, columns = blocks[n]
        rows = head_rows(head, width)
        return head_terms(
            head, span, columns.start, tile_rows, keys, values, bias, query_t_ref[rows, columns], grad_t_ref[rows, columns]
        )

    def store(n, raw):
        head, columns = blocks[n]
        place = slice(n * span, (n + 1) * span)
        weights_ref[:, place] = jnp.exp2(raw[0] * factor - near_ref[head : head + 1, columns])
        dprobs_ref[:, place] = raw[1]

    staggered(len(blocks), (terms, store), (0, 1))


def products_of(blocks, queries, query_t_ref, grad_t_ref, keys_t, query_sum_ref, before_ref, sums_ref, scale):
    width = query_t_ref.shape[0]
    partial = {}

    def products(n, ready):
        head, columns = blocks[n]
        probs, dscores = ready
        rows = head_rows(head, width)
        key_part = dot(query_t_ref[rows, columns], dscores, NT)
        value_part = dot(grad_t_ref[rows, columns], probs, NT)
        piece = dot(keys_t[rows, :], dscores, NN)
        if before_ref is not None:
            piece += before_ref[rows, columns]
        query_sum_ref[rows, columns] = piece
        if columns.start > 0:
            before = partial.pop(head)
            key_part, value_part = before[0] + key_part, before[1] + value_part
        if columns.stop < queries:
            partial[head] = (key_part, value_part)
        else:
            sums_ref[rows, :] = key_part * scale
            sums_ref[width + rows.start : width + rows.stop, :] = value_part

    return products


def third_kernel(span, scale, near_ref, across_ref, chunk_ref, query_t_ref, grad_t_ref, weights_ref, dprobs_ref,
                 out_ref, query_sum_ref, ends_ref, sums_ref, shrink_ref):
    width, queries = query_t_ref.shape
    rows = queries // 2
    turned = jnp.concatenate((across_ref[:, rows:], across_ref[:, :rows]), axis=1)
    top = jnp.maximum(near_ref[:H, :], turned[:H, :])
    near, across = jnp.exp2(near_ref[:H, :] - top), jnp.exp2(turned[:H, :] - top)
    total = near + across
    lse = top + jnp.log2(total)
    ends_ref[:H, :] = lse
    ends_ref[H:, :] = (near * near_ref[H:, :] + across * turned[H:, :]) / total
    shrink_ref[...] = jnp.exp2(near_ref[:H, :] - lse)
    keys_t = chunk_ref[:, :width].T
    blocks = block_list(queries, span)

    def rounded(n):
        head, columns = blocks[n]
        place = slice(n * span, (n + 1) * span)
        probs = weights_ref[:, place] * shrink_ref[head : head + 1, columns]
        dscores = probs * (dprobs_ref[:, place] - ends_ref[H + head : H + head + 1, columns])
        return probs.astype(BF16), dscores.astype(BF16)

    products = products_of(blocks, queries, query_t_ref, grad_t_ref, keys_t, query_sum_ref, None, sums_ref, scale)
    staggered(len(blocks), (rounded, products), (0, 1))
    out_ref[...] = sums_ref[...].T.astype(out_ref.dtype)


def fourth_kernel(cams, span, tile_rows, factor, scale, where_ref, ends_ref, before_ref, chunk_ref, bias_ref, query_t_ref,
                  grad_t_ref, out_ref, keep_ref, *refs):
    turn_refs, (query_sum_ref, sums_ref, whole_ref) = refs[: cams - 1], refs[cams - 1 :]
    width, queries = query_t_ref.shape
    keys, values = chunk_of(chunk_ref, width)
    keys_t = chunk_ref[:, :width].T
    bias = bias_ref[: chunk_ref.shape[0], :]
    blocks = block_list(queries, span)

    def terms(n):
        head, columns = blocks[n]
        rows = head_rows(head, width)
        return head_terms(
            head, span, columns.start, tile_rows, keys, values, bias, query_t_ref[rows, columns], grad_t_ref[rows, columns]
        )

    def rounded(n, raw):
        head, columns = blocks[n]
        probs = jnp.exp2(raw[0] * factor - ends_ref[head : head + 1, columns])
        dscores = probs * (raw[1] - ends_ref[H + head : H + head + 1, columns])
        return probs.astype(BF16), dscores.astype(BF16)

    products = products_of(blocks, queries, query_t_ref, grad_t_ref, keys_t, query_sum_ref, before_ref, sums_ref, scale)
    staggered(len(blocks), (terms, rounded, products), (0, 1, 2))
    out_ref[...] = sums_ref[...].T.astype(out_ref.dtype)
    whole_ref[...] = query_sum_ref[...].T * scale
    count = keep_ref.shape[0] // 2
    for shift, ref in enumerate((keep_ref, *turn_refs)):
        piece = lax.rem(where_ref[1] + shift, cams)
        for side in range(2):
            start = pl.multiple_of(side * (queries // 2) + piece * count, 16)
            ref[side * count : (side + 1) * count, :] = whole_ref[pl.ds(start, count), :].astype(ref.dtype)


def run(kernel, outs, args, scratch=(), smem=0, flops=0, space=pltpu.VMEM):
    size = lambda a: math.prod(a.shape) * a.dtype.itemsize
    moved = sum(size(a) for a in args) + sum(size(a) for a in outs)
    vmem = pl.BlockSpec(memory_space=pltpu.VMEM)
    return pl.pallas_call(
        kernel,
        out_shape=tuple(outs),
        in_specs=[pl.BlockSpec(memory_space=pltpu.SMEM)] * smem + [pl.BlockSpec(memory_space=space)] * (len(args) - smem),
        out_specs=tuple([vmem] * len(outs)),
        scratch_shapes=list(scratch),
        cost_estimate=pl.CostEstimate(flops=flops, bytes_accessed=moved, transcendentals=flops // 64),
        compiler_params=pltpu.CompilerParams(vmem_limit_bytes=40 * 1024 * 1024),
    )(*args)


def combine(parts, factor):
    top = functools.reduce(jnp.maximum, [part[:H] for part in parts])
    shrink = [jnp.exp2((part[:H] - top) * factor) for part in parts]
    total = sum(s * part[H : 2 * H] for s, part in zip(shrink, parts))
    product = sum(s * part[2 * H :] for s, part in zip(shrink, parts))
    return jnp.concatenate((top * factor + jnp.log2(total), product / total), axis=0)


def shards(queries, keys, values, grad_out, visible, counts):
    rows, width = queries.shape
    shard_rows = keys.shape[0]
    head_dim = width // H
    scale = 1.0 / math.sqrt(head_dim)
    factor = scale * math.log2(math.e)
    tiles, cams = lax.axis_size("tile"), lax.axis_size("cam")
    tile, cam = lax.axis_index("tile"), lax.axis_index("cam")
    blocks = counts.shape[0]
    block_keys = shard_rows * tiles // blocks
    own_tiles = visible.shape[0]
    tile_rows = rows // own_tiles
    orders = step_orders(tiles)
    masks = [slot_masks(order) for order in orders]
    span = 256

    def across(x, hop):
        pairs = [(c * tiles + t, c * tiles + (t ^ hop(c))) for c in range(cams) for t in range(tiles)]
        return lax.ppermute(x, ("cam", "tile"), pairs)

    def step(x, k):
        return across(x, lambda c: orders[c % 2][k])

    def swap_half(x):
        return across(x, lambda c: tiles // 2)

    def turn(x, shift):
        return lax.ppermute(x, "cam", [(c, (c + shift) % cams) for c in range(cams)])

    steps = len(orders[0])
    shape = jax.ShapeDtypeStruct
    piece_rows = 2 * rows // cams
    where = jnp.stack((tile, cam)).astype(jnp.int32)
    lanes = -(-blocks // LANES) * LANES
    fixed = (keys, values, queries, grad_out, visible, counts.reshape(1, blocks))
    held, query_near, grad_near, message, table = run(
        functools.partial(start_kernel, cams),
        (
            shape((shard_rows, 2 * width), BF16),
            shape((rows, width), BF16),
            shape((rows, width), BF16),
            shape((piece_rows + 16, width), BF16),
            shape((LANES, lanes), BF16),
        ),
        (where, *(pltpu.with_memory_space_constraint(x, pltpu.HBM) for x in fixed)),
        scratch=(
            pltpu.VMEM(visible.shape, visible.dtype),
            pltpu.VMEM((1, blocks), counts.dtype),
            pltpu.SemaphoreType.DMA((len(fixed),)),
        ),
        smem=1,
        space=pltpu.HBM,
    )
    received = swap_half(message)
    for k in range(steps - 2):
        held = jnp.concatenate((held, step(held, k)), axis=0)
    nearer = step(held, steps - 2)
    farther = step(held, steps - 1)
    farthest = across(held, lambda c: orders[c % 2][-1] ^ orders[c % 2][-2])
    pieces = [received] + [turn(received, shift) for shift in range(1, cams)]
    held = jnp.concatenate((held, nearer), axis=0)
    last = jnp.concatenate((farther, farthest), axis=0)

    all_rows = 2 * rows
    chunk = held.shape[0]
    work = 2 * all_rows * chunk * width
    stats, query_t, grad_t, bias = run(
        functools.partial(first_kernel, cams, blocks, masks, shard_rows, block_keys, span, tile_rows, factor),
        (
            shape((3 * H, all_rows), F32),
            shape((width, all_rows), BF16),
            shape((width, all_rows), BF16),
            shape((2 * chunk, LANES), BF16),
        ),
        (where, query_near, grad_near, *pieces, held, table),
        scratch=(pltpu.VMEM((2 * rows, width), BF16), pltpu.VMEM((LANES, lanes), BF16)),
        smem=1,
        flops=8 * work,
    )
    (stats,) = run(
        functools.partial(second_kernel, span, tile_rows, factor),
        (shape((3 * H, all_rows), F32),),
        (last, bias, query_t, grad_t, stats),
        flops=8 * work,
    )
    near = combine([stats] + [turn(stats, shift) for shift in range(1, cams)], factor)
    opposite = swap_half(near)
    weights, dprobs = run(
        functools.partial(near_kernel, span, tile_rows, factor),
        (shape((chunk, H * all_rows), F32), shape((chunk, H * all_rows), F32)),
        (near, last, bias, query_t, grad_t),
        flops=8 * work,
    )

    scratch = (pltpu.VMEM((2 * width, chunk), F32),)
    sent, query_sum, ends = run(
        functools.partial(third_kernel, span, scale),
        (shape((chunk, 2 * width), BF16), shape((width, all_rows), F32), shape((2 * H, all_rows), F32)),
        (near, opposite, last, query_t, grad_t, weights, dprobs),
        scratch=(*scratch, pltpu.VMEM((H, all_rows), F32)),
        flops=20 * work,
    )
    got = step(sent, steps - 1)
    part = rows // cams
    kept, query_part, *to_turn = run(
        functools.partial(fourth_kernel, cams, span, tile_rows, factor, scale),
        (
            shape((chunk, 2 * width), F32),
            shape((2 * part, width), F32),
            *(shape((2 * part, width), BF16) for _ in range(1, cams)),
        ),
        (where, ends, query_sum, held, bias, query_t, grad_t),
        scratch=(pltpu.VMEM((width, all_rows), F32), *scratch, pltpu.VMEM((all_rows, width), F32)),
        smem=1,
        flops=20 * work,
    )
    for shift in range(1, cams):
        query_part = query_part + turn(to_turn[shift - 1], shift).astype(F32)
    query_far = query_part[part:].astype(BF16)
    query_got = swap_half(query_far)
    sums = kept + got.astype(F32)
    slots = [sums[k * shard_rows : (k + 1) * shard_rows] for k in range(chunk // shard_rows)]
    outs = [slot.astype(BF16) for slot in slots[1:]]
    owned = slots[0]
    for k, out in enumerate(outs):
        owned = owned + across(out, lambda c: masks[c % 2][k + 1]).astype(F32)
    owned = owned.astype(BF16)
    mine = (query_part[:part] + query_got.astype(F32)).astype(BF16)
    parts = [mine] + [turn(mine, shift) for shift in range(1, cams)]
    ordered = []
    for k in range(cams):
        source = (cam + cams - k) % cams
        ordered.append(functools.reduce(lambda x, s: jnp.where(source == s, parts[s], x), range(1, cams), parts[0]))
    query_part = jnp.concatenate(ordered, axis=0)
    return (query_part, owned[:, :width], owned[:, width:])


def solution(mesh):
    in_specs = (
        P("tile", None),
        P(("cam", "tile"), None),
        P(("cam", "tile"), None),
        P("tile", None),
        P("tile", "cam"),
        P("cam"),
    )
    out_specs = (P("tile", None), P(("cam", "tile"), None), P(("cam", "tile"), None))

    return jax.shard_map(shards, mesh=mesh, in_specs=in_specs, out_specs=out_specs, check_vma=False)
```

```python
import functools
import math

import jax
import jax.numpy as jnp
from jax import lax
from jax.experimental import pallas as pl
from jax.experimental.pallas import tpu as pltpu
from jax.sharding import PartitionSpec as P


H = 8
LANES = 128
FAR = -1e30
BF16 = jnp.bfloat16
F32 = jnp.float32


def dot(a, b, dims):
    return lax.dot_general(a, b, (dims, ((), ())), preferred_element_type=F32)


NN = ((1,), (0,))
NT = ((1,), (1,))


def step_orders(tiles):
    bits = []
    bit = 1
    while bit < tiles // 2:
        bits.append(bit)
        bit *= 2
    return (tuple(bits[:1] + bits[:0:-1]), tuple(bits[::-1]))


def slot_masks(order):
    masks = [0]
    for bit in order:
        masks = masks + [mask ^ bit for mask in masks]
    return masks


def start_kernel(cams, key_ref, value_ref, query_ref, grad_ref, seen_ref, limit_ref, pair_ref, query_out,
                 grad_out, message_ref, table_ref, seen_vmem, limit_vmem, sems):
    rows, width = query_ref.shape
    own_tiles, blocks = seen_ref.shape
    moves = (
        (query_ref, query_out),
        (grad_ref, grad_out),
        (seen_ref, seen_vmem),
        (limit_ref, limit_vmem),
        (key_ref, pair_ref.at[:, :width]),
        (value_ref, pair_ref.at[:, width:]),
    )
    copies = [pltpu.make_async_copy(source, target, sems.at[k]) for k, (source, target) in enumerate(moves)]
    for copy in copies:
        copy.start()
    piece_rows = 2 * rows // cams
    message_ref[piece_rows:, :] = jnp.zeros((16, width), BF16)
    table_ref[...] = jnp.zeros(table_ref.shape, BF16)
    for copy in copies:
        copy.wait()
    for piece in range(cams):

        @pl.when(lax.axis_index("cam") == piece)
        def _(first=piece * piece_rows):
            source, at = (query_out, first) if first < rows else (grad_out, first - rows)
            message_ref[:piece_rows, :] = source[at : at + piece_rows, :]

    seen = seen_vmem[...].astype(F32).astype(BF16)
    message_ref[piece_rows : piece_rows + own_tiles, :blocks] = seen
    table_ref[:own_tiles, :blocks] = seen
    table_ref[LANES - 1 : LANES, :blocks] = limit_vmem[...].astype(F32).astype(BF16)


def build_bias(table_ref, bias_ref, masks, shard_rows, block_keys):
    tile, cam = lax.axis_index("tile"), lax.axis_index("cam")
    per_shard = shard_rows // block_keys
    lanes = table_ref.shape[1]
    table = table_ref[...]
    lane = lax.broadcasted_iota(jnp.int32, (shard_rows, lanes), 1)
    row = lax.broadcasted_iota(jnp.int32, (shard_rows, lanes), 0)
    place = lax.broadcasted_iota(jnp.int32, (shard_rows, LANES), 0) % block_keys
    column = lax.broadcasted_iota(jnp.int32, (shard_rows, LANES), 1)
    for slot in range(len(masks[0])):
        mask = jnp.where(cam % 2 == 0, masks[0][slot], masks[1][slot])
        block = (tile ^ mask) * per_shard + row // block_keys
        picked = dot((lane == block).astype(F32).astype(BF16), table, NT)
        count = picked[:, LANES - 1 : LANES]
        allowed = (picked > 0.5) & (place.astype(F32) < count)
        bias = jnp.where(allowed | (column == LANES - 1), 0.0, FAR)
        bias_ref[slot * shard_rows : (slot + 1) * shard_rows, :] = bias.astype(BF16)


def head_terms(head, span, first, tile_rows, keys, values, bias, query_t, grad_t):
    size = query_t.shape[0]
    half, inside = head * size // LANES, head * size % LANES

    def alone(rows):
        parts = [jnp.zeros((inside, span), BF16)] if inside else []
        parts.append(rows)
        if inside + size < LANES:
            parts.append(jnp.zeros((LANES - inside - size, span), BF16))
        return jnp.concatenate(parts, axis=0)

    tile_of = (lax.broadcasted_iota(jnp.int32, (LANES, span), 1) + first) // tile_rows
    hot = (lax.broadcasted_iota(jnp.int32, (LANES, span), 0) == tile_of).astype(F32).astype(BF16)
    right = jnp.concatenate((alone(query_t), hot), axis=0)
    left = jnp.concatenate((keys[half], bias), axis=1)
    return dot(left, right, NN), dot(values[half], alone(grad_t), NN)


def chunk_of(ref, width):
    keys = [ref[:, k * LANES : (k + 1) * LANES] for k in range(width // LANES)]
    values = [ref[:, width + k * LANES : width + (k + 1) * LANES] for k in range(width // LANES)]
    return keys, values


def stats_of(ref, bias, query_t_ref, grad_t_ref, before_ref, stats_ref, span, tile_rows, factor):
    width, queries = query_t_ref.shape
    keys, values = chunk_of(ref, width)
    for head in range(H):
        rows = slice(head * width // H, (head + 1) * width // H)
        for first in range(0, queries, span):
            columns = slice(first, first + span)
            scores, dprobs = head_terms(
                head, span, first, tile_rows, keys, values, bias, query_t_ref[rows, columns], grad_t_ref[rows, columns]
            )
            top = jnp.max(scores, axis=0, keepdims=True)
            if before_ref is not None:
                old_top = before_ref[head : head + 1, columns]
                top = jnp.maximum(top, old_top)
            weights = jnp.exp2((scores - top) * factor)
            total = jnp.sum(weights, axis=0, keepdims=True)
            product = jnp.sum(weights * dprobs, axis=0, keepdims=True)
            if before_ref is not None:
                shrink = jnp.exp2((old_top - top) * factor)
                total = total + shrink * before_ref[H + head : H + head + 1, columns]
                product = product + shrink * before_ref[2 * H + head : 2 * H + head + 1, columns]
            stats_ref[head : head + 1, columns] = top
            stats_ref[H + head : H + head + 1, columns] = total
            stats_ref[2 * H + head : 2 * H + head + 1, columns] = product


def first_kernel(cams, blocks, masks, shard_rows, block_keys, span, tile_rows, factor, query_ref, grad_ref, *refs):
    pieces, (chunk_ref, table_ref), outs = refs[:cams], refs[cams : cams + 2], refs[cams + 2 :]
    stats_ref, query_t_ref, grad_t_ref, bias_ref, far_ref, full_table_ref = outs
    rows, _ = query_ref.shape
    own_tiles = rows // tile_rows
    note = slice(2 * rows // cams, 2 * rows // cams + own_tiles)
    full_table_ref[...] = table_ref[...]
    full_table_ref[own_tiles : 2 * own_tiles, :blocks] = pieces[0][note, :blocks]
    build_bias(full_table_ref, bias_ref, masks, shard_rows, block_keys)
    piece_rows = 2 * rows // cams
    for shift in range(cams):
        piece = lax.rem(lax.axis_index("cam") + cams - shift, cams)
        start = pl.multiple_of(piece * piece_rows, 16)
        far_ref[pl.ds(start, piece_rows), :] = pieces[shift][:piece_rows, :]
    query_t_ref[:, :rows] = query_ref[...].T
    query_t_ref[:, rows:] = far_ref[:rows, :].T
    grad_t_ref[:, :rows] = grad_ref[...].T
    grad_t_ref[:, rows:] = far_ref[rows:, :].T
    bias = bias_ref[: chunk_ref.shape[0], :]
    stats_of(chunk_ref, bias, query_t_ref, grad_t_ref, None, stats_ref, span, tile_rows, factor)


def second_kernel(span, tile_rows, factor, chunk_ref, bias_ref, query_t_ref, grad_t_ref, before_ref, stats_ref):
    bias = bias_ref[chunk_ref.shape[0] :, :]
    stats_of(chunk_ref, bias, query_t_ref, grad_t_ref, before_ref, stats_ref, span, tile_rows, factor)


def head_rows(head, width):
    return slice(head * width // H, (head + 1) * width // H)


def staggered(count, stages, lags):
    results = [{} for _ in stages]
    total = sum(lags)
    for n in range(count + total):
        at = n
        for k, stage in enumerate(stages):
            at -= lags[k]
            if 0 <= at < count:
                results[k][at] = stage(at) if k == 0 else stage(at, results[k - 1].pop(at))


def block_list(queries, span):
    return [(head, slice(first, first + span)) for head in range(H) for first in range(0, queries, span)]


def near_kernel(span, tile_rows, factor, near_ref, chunk_ref, bias_ref, query_t_ref, grad_t_ref, weights_ref, dprobs_ref):
    width, queries = query_t_ref.shape
    keys, values = chunk_of(chunk_ref, width)
    bias = bias_ref[chunk_ref.shape[0] :, :]
    blocks = block_list(queries, span)

    def terms(n):
        head, columns = blocks[n]
        rows = head_rows(head, width)
        return head_terms(
            head, span, columns.start, tile_rows, keys, values, bias, query_t_ref[rows, columns], grad_t_ref[rows, columns]
        )

    def store(n, raw):
        head, columns = blocks[n]
        place = slice(n * span, (n + 1) * span)
        weights_ref[:, place] = jnp.exp2(raw[0] * factor - near_ref[head : head + 1, columns])
        dprobs_ref[:, place] = raw[1]

    staggered(len(blocks), (terms, store), (0, 1))


def products_of(blocks, queries, query_t_ref, grad_t_ref, keys_t, query_sum_ref, before_ref, out_ref, scale):
    width = query_t_ref.shape[0]
    partial, done = {}, {}

    def products(n, ready):
        head, columns = blocks[n]
        probs, dscores = ready
        rows = head_rows(head, width)
        key_part = dot(query_t_ref[rows, columns], dscores, NT)
        value_part = dot(grad_t_ref[rows, columns], probs, NT)
        piece = dot(keys_t[rows, :], dscores, NN)
        if before_ref is not None:
            piece += before_ref[rows, columns]
        query_sum_ref[rows, columns] = piece
        if columns.start > 0:
            before = partial.pop(head)
            key_part, value_part = before[0] + key_part, before[1] + value_part
        if columns.stop < queries:
            partial[head] = (key_part, value_part)
        else:
            done[head] = (key_part * scale, value_part)
        if rows.stop % LANES == 0 and head in done:
            heads = sorted(done)
            for side in range(2):
                group = jnp.concatenate([done[h][side] for h in heads], axis=0)
                place = side * width + rows.stop - LANES
                out_ref[:, place : place + LANES] = group.T.astype(out_ref.dtype)
            done.clear()

    return products


def third_kernel(span, scale, near_ref, across_ref, chunk_ref, query_t_ref, grad_t_ref, weights_ref, dprobs_ref,
                 out_ref, query_sum_ref, ends_ref, shrink_ref):
    width, queries = query_t_ref.shape
    rows = queries // 2
    turned = jnp.concatenate((across_ref[:, rows:], across_ref[:, :rows]), axis=1)
    top = jnp.maximum(near_ref[:H, :], turned[:H, :])
    near, across = jnp.exp2(near_ref[:H, :] - top), jnp.exp2(turned[:H, :] - top)
    total = near + across
    lse = top + jnp.log2(total)
    ends_ref[:H, :] = lse
    ends_ref[H:, :] = (near * near_ref[H:, :] + across * turned[H:, :]) / total
    shrink_ref[...] = jnp.exp2(near_ref[:H, :] - lse)
    keys_t = chunk_ref[:, :width].T
    blocks = block_list(queries, span)

    def rounded(n):
        head, columns = blocks[n]
        place = slice(n * span, (n + 1) * span)
        probs = weights_ref[:, place] * shrink_ref[head : head + 1, columns]
        dscores = probs * (dprobs_ref[:, place] - ends_ref[H + head : H + head + 1, columns])
        return probs.astype(BF16), dscores.astype(BF16)

    products = products_of(blocks, queries, query_t_ref, grad_t_ref, keys_t, query_sum_ref, None, out_ref, scale)
    staggered(len(blocks), (rounded, products), (0, 1))


def fourth_kernel(cams, span, tile_rows, factor, scale, ends_ref, before_ref, chunk_ref, bias_ref, query_t_ref,
                  grad_t_ref, out_ref, keep_ref, *refs):
    turn_refs, (query_sum_ref, whole_ref) = refs[: cams - 1], refs[cams - 1 :]
    width, queries = query_t_ref.shape
    keys, values = chunk_of(chunk_ref, width)
    keys_t = chunk_ref[:, :width].T
    bias = bias_ref[: chunk_ref.shape[0], :]
    blocks = block_list(queries, span)

    def terms(n):
        head, columns = blocks[n]
        rows = head_rows(head, width)
        return head_terms(
            head, span, columns.start, tile_rows, keys, values, bias, query_t_ref[rows, columns], grad_t_ref[rows, columns]
        )

    def rounded(n, raw):
        head, columns = blocks[n]
        probs = jnp.exp2(raw[0] * factor - ends_ref[head : head + 1, columns])
        dscores = probs * (raw[1] - ends_ref[H + head : H + head + 1, columns])
        return probs.astype(BF16), dscores.astype(BF16)

    products = products_of(blocks, queries, query_t_ref, grad_t_ref, keys_t, query_sum_ref, before_ref, out_ref, scale)
    staggered(len(blocks), (terms, rounded, products), (0, 1, 2))
    count = keep_ref.shape[0] // 2
    if count % LANES:
        whole_ref[...] = query_sum_ref[...].T
    for shift, ref in enumerate((keep_ref, *turn_refs)):
        piece = lax.rem(lax.axis_index("cam") + shift, cams)
        for side in range(2):
            start = pl.multiple_of(side * (queries // 2) + piece * count, count)
            if count % LANES:
                part = whole_ref[pl.ds(start, count), :]
            else:
                part = query_sum_ref[:, pl.ds(start, count)].T
            ref[side * count : (side + 1) * count, :] = (part * scale).astype(ref.dtype)


def run(kernel, outs, args, scratch=(), flops=0, space=pltpu.VMEM):
    size = lambda a: math.prod(a.shape) * a.dtype.itemsize
    moved = sum(size(a) for a in args) + sum(size(a) for a in outs)
    vmem = pl.BlockSpec(memory_space=pltpu.VMEM)
    return pl.pallas_call(
        kernel,
        out_shape=tuple(outs),
        in_specs=[pl.BlockSpec(memory_space=space)] * len(args),
        out_specs=tuple([vmem] * len(outs)),
        scratch_shapes=list(scratch),
        cost_estimate=pl.CostEstimate(flops=flops, bytes_accessed=moved, transcendentals=flops // 64),
        compiler_params=pltpu.CompilerParams(vmem_limit_bytes=40 * 1024 * 1024),
    )(*args)


def combine(parts, factor):
    top = functools.reduce(jnp.maximum, [part[:H] for part in parts])
    shrink = [jnp.exp2((part[:H] - top) * factor) for part in parts]
    total = sum(s * part[H : 2 * H] for s, part in zip(shrink, parts))
    product = sum(s * part[2 * H :] for s, part in zip(shrink, parts))
    return jnp.concatenate((top * factor + jnp.log2(total), product / total), axis=0)


def shards(queries, keys, values, grad_out, visible, counts):
    rows, width = queries.shape
    shard_rows = keys.shape[0]
    head_dim = width // H
    scale = 1.0 / math.sqrt(head_dim)
    factor = scale * math.log2(math.e)
    tiles, cams = lax.axis_size("tile"), lax.axis_size("cam")
    cam = lax.axis_index("cam")
    blocks = counts.shape[0]
    block_keys = shard_rows * tiles // blocks
    own_tiles = visible.shape[0]
    tile_rows = rows // own_tiles
    orders = step_orders(tiles)
    masks = [slot_masks(order) for order in orders]
    span = 256

    def across(x, hop):
        pairs = [(c * tiles + t, c * tiles + (t ^ hop(c))) for c in range(cams) for t in range(tiles)]
        return lax.ppermute(x, ("cam", "tile"), pairs)

    def step(x, k):
        return across(x, lambda c: orders[c % 2][k])

    def swap_half(x):
        return across(x, lambda c: tiles // 2)

    def turn(x, shift):
        return lax.ppermute(x, "cam", [(c, (c + shift) % cams) for c in range(cams)])

    steps = len(orders[0])
    shape = jax.ShapeDtypeStruct
    piece_rows = 2 * rows // cams
    lanes = -(-blocks // LANES) * LANES
    fixed = (keys, values, queries, grad_out, visible, counts.reshape(1, blocks))
    held, query_near, grad_near, message, table = run(
        functools.partial(start_kernel, cams),
        (
            shape((shard_rows, 2 * width), BF16),
            shape((rows, width), BF16),
            shape((rows, width), BF16),
            shape((piece_rows + 16, width), BF16),
            shape((LANES, lanes), BF16),
        ),
        tuple(pltpu.with_memory_space_constraint(x, pltpu.HBM) for x in fixed),
        scratch=(
            pltpu.VMEM(visible.shape, visible.dtype),
            pltpu.VMEM((1, blocks), counts.dtype),
            pltpu.SemaphoreType.DMA((len(fixed),)),
        ),
        space=pltpu.HBM,
    )
    received = swap_half(message)
    for k in range(steps - 2):
        held = jnp.concatenate((held, step(held, k)), axis=0)
    nearer = step(held, steps - 2)
    farther = step(held, steps - 1)
    farthest = across(held, lambda c: orders[c % 2][-1] ^ orders[c % 2][-2])
    pieces = [received] + [turn(received, shift) for shift in range(1, cams)]
    held = jnp.concatenate((held, nearer), axis=0)
    last = jnp.concatenate((farther, farthest), axis=0)

    all_rows = 2 * rows
    chunk = held.shape[0]
    work = 2 * all_rows * chunk * width
    stats, query_t, grad_t, bias = run(
        functools.partial(first_kernel, cams, blocks, masks, shard_rows, block_keys, span, tile_rows, factor),
        (
            shape((3 * H, all_rows), F32),
            shape((width, all_rows), BF16),
            shape((width, all_rows), BF16),
            shape((2 * chunk, LANES), BF16),
        ),
        (query_near, grad_near, *pieces, held, table),
        scratch=(pltpu.VMEM((2 * rows, width), BF16), pltpu.VMEM((LANES, lanes), BF16)),
            flops=8 * work,
    )
    (stats,) = run(
        functools.partial(second_kernel, span, tile_rows, factor),
        (shape((3 * H, all_rows), F32),),
        (last, bias, query_t, grad_t, stats),
        flops=8 * work,
    )
    near = combine([stats] + [turn(stats, shift) for shift in range(1, cams)], factor)
    opposite = swap_half(near)
    weights, dprobs = run(
        functools.partial(near_kernel, span, tile_rows, factor),
        (shape((chunk, H * all_rows), F32), shape((chunk, H * all_rows), F32)),
        (near, last, bias, query_t, grad_t),
        flops=8 * work,
    )

    sent, query_sum, ends = run(
        functools.partial(third_kernel, span, scale),
        (shape((chunk, 2 * width), BF16), shape((width, all_rows), F32), shape((2 * H, all_rows), F32)),
        (near, opposite, last, query_t, grad_t, weights, dprobs),
        scratch=(pltpu.VMEM((H, all_rows), F32),),
        flops=20 * work,
    )
    got = step(sent, steps - 1)
    part = rows // cams
    kept, query_part, *to_turn = run(
        functools.partial(fourth_kernel, cams, span, tile_rows, factor, scale),
        (
            shape((chunk, 2 * width), F32),
            shape((2 * part, width), F32),
            *(shape((2 * part, width), BF16) for _ in range(1, cams)),
        ),
        (ends, query_sum, held, bias, query_t, grad_t),
        scratch=(pltpu.VMEM((width, all_rows), F32), pltpu.VMEM((all_rows, width), F32)),
            flops=20 * work,
    )
    for shift in range(1, cams):
        query_part = query_part + turn(to_turn[shift - 1], shift).astype(F32)
    query_far = query_part[part:].astype(BF16)
    query_got = swap_half(query_far)
    sums = kept + got.astype(F32)
    slots = [sums[k * shard_rows : (k + 1) * shard_rows] for k in range(chunk // shard_rows)]
    outs = [slot.astype(BF16) for slot in slots[1:]]
    owned = slots[0]
    for k in range(len(outs), 0, -1):
        owned = owned + across(outs[k - 1], lambda c: masks[c % 2][k]).astype(F32)
    owned = owned.astype(BF16)
    mine = (query_part[:part] + query_got.astype(F32)).astype(BF16)
    parts = [mine] + [turn(mine, shift) for shift in range(1, cams)]
    ordered = []
    for k in range(cams):
        source = (cam + cams - k) % cams
        ordered.append(functools.reduce(lambda x, s: jnp.where(source == s, parts[s], x), range(1, cams), parts[0]))
    query_part = jnp.concatenate(ordered, axis=0)
    return (query_part, owned[:, :width], owned[:, width:])


def solution(mesh):
    in_specs = (
        P("tile", None),
        P(("cam", "tile"), None),
        P(("cam", "tile"), None),
        P("tile", None),
        P("tile", "cam"),
        P("cam"),
    )
    out_specs = (P("tile", None), P(("cam", "tile"), None), P(("cam", "tile"), None))

    return jax.shard_map(shards, mesh=mesh, in_specs=in_specs, out_specs=out_specs, check_vma=False)
```

```python
import functools
import math

import jax
import jax.numpy as jnp
from jax import lax
from jax.experimental import pallas as pl
from jax.experimental.pallas import tpu as pltpu
from jax.sharding import PartitionSpec as P


H = 8
LANES = 128
FAR = -1e30
BF16 = jnp.bfloat16
F32 = jnp.float32


def dot(a, b, dims):
    return lax.dot_general(a, b, (dims, ((), ())), preferred_element_type=F32)


NN = ((1,), (0,))
NT = ((1,), (1,))


def step_orders(tiles):
    bits = []
    bit = 1
    while bit < tiles // 2:
        bits.append(bit)
        bit *= 2
    return (tuple(bits[:1] + bits[:0:-1]), tuple(bits[::-1]))


def slot_masks(order):
    masks = [0]
    for bit in order:
        masks = masks + [mask ^ bit for mask in masks]
    return masks


def start_kernel(cams, key_ref, value_ref, query_ref, grad_ref, seen_ref, limit_ref, pair_ref, query_out,
                 grad_out, message_ref, table_ref, seen_vmem, limit_vmem, sems):
    rows, width = query_ref.shape
    own_tiles, blocks = seen_ref.shape
    moves = (
        (query_ref, query_out),
        (grad_ref, grad_out),
        (seen_ref, seen_vmem),
        (limit_ref, limit_vmem),
        (key_ref, pair_ref.at[:, :width]),
        (value_ref, pair_ref.at[:, width:]),
    )
    copies = [pltpu.make_async_copy(source, target, sems.at[k]) for k, (source, target) in enumerate(moves)]
    for copy in copies:
        copy.start()
    piece_rows = 2 * rows // cams
    message_ref[piece_rows:, :] = jnp.zeros((16, width), BF16)
    table_ref[...] = jnp.zeros(table_ref.shape, BF16)
    for copy in copies:
        copy.wait()
    for piece in range(cams):

        @pl.when(lax.axis_index("cam") == piece)
        def _(first=piece * piece_rows):
            source, at = (query_out, first) if first < rows else (grad_out, first - rows)
            message_ref[:piece_rows, :] = source[at : at + piece_rows, :]

    seen = seen_vmem[...].astype(F32).astype(BF16)
    message_ref[piece_rows : piece_rows + own_tiles, :blocks] = seen
    table_ref[:own_tiles, :blocks] = seen
    table_ref[LANES - 1 : LANES, :blocks] = limit_vmem[...].astype(F32).astype(BF16)


def build_bias(table_ref, bias_ref, masks, shard_rows, block_keys):
    tile, cam = lax.axis_index("tile"), lax.axis_index("cam")
    per_shard = shard_rows // block_keys
    lanes = table_ref.shape[1]
    table = table_ref[...]
    lane = lax.broadcasted_iota(jnp.int32, (shard_rows, lanes), 1)
    row = lax.broadcasted_iota(jnp.int32, (shard_rows, lanes), 0)
    place = lax.broadcasted_iota(jnp.int32, (shard_rows, LANES), 0) % block_keys
    column = lax.broadcasted_iota(jnp.int32, (shard_rows, LANES), 1)
    for slot in range(len(masks[0])):
        mask = jnp.where(cam % 2 == 0, masks[0][slot], masks[1][slot])
        block = (tile ^ mask) * per_shard + row // block_keys
        picked = dot((lane == block).astype(F32).astype(BF16), table, NT)
        count = picked[:, LANES - 1 : LANES]
        allowed = (picked > 0.5) & (place.astype(F32) < count)
        bias = jnp.where(allowed | (column == LANES - 1), 0.0, FAR)
        bias_ref[slot * shard_rows : (slot + 1) * shard_rows, :] = bias.astype(BF16)


def head_terms(head, span, first, tile_rows, keys, values, bias, query_t, grad_t):
    size = query_t.shape[0]
    half, inside = head * size // LANES, head * size % LANES

    def alone(rows):
        parts = [jnp.zeros((inside, span), BF16)] if inside else []
        parts.append(rows)
        if inside + size < LANES:
            parts.append(jnp.zeros((LANES - inside - size, span), BF16))
        return jnp.concatenate(parts, axis=0)

    tile_of = (lax.broadcasted_iota(jnp.int32, (LANES, span), 1) + first) // tile_rows
    hot = (lax.broadcasted_iota(jnp.int32, (LANES, span), 0) == tile_of).astype(F32).astype(BF16)
    right = jnp.concatenate((alone(query_t), hot), axis=0)
    left = jnp.concatenate((keys[half], bias), axis=1)
    return dot(left, right, NN), dot(values[half], alone(grad_t), NN)


def chunk_of(ref, width):
    keys = [ref[:, k * LANES : (k + 1) * LANES] for k in range(width // LANES)]
    values = [ref[:, width + k * LANES : width + (k + 1) * LANES] for k in range(width // LANES)]
    return keys, values


def stats_of(ref, bias, query_t_ref, grad_t_ref, before_ref, stats_ref, span, tile_rows, factor):
    width, queries = query_t_ref.shape
    keys, values = chunk_of(ref, width)
    for head in range(H):
        rows = slice(head * width // H, (head + 1) * width // H)
        for first in range(0, queries, span):
            columns = slice(first, first + span)
            scores, dprobs = head_terms(
                head, span, first, tile_rows, keys, values, bias, query_t_ref[rows, columns], grad_t_ref[rows, columns]
            )
            top = jnp.max(scores, axis=0, keepdims=True)
            if before_ref is not None:
                old_top = before_ref[head : head + 1, columns]
                top = jnp.maximum(top, old_top)
            weights = jnp.exp2((scores - top) * factor)
            total = jnp.sum(weights, axis=0, keepdims=True)
            product = jnp.sum(weights * dprobs, axis=0, keepdims=True)
            if before_ref is not None:
                shrink = jnp.exp2((old_top - top) * factor)
                total = total + shrink * before_ref[H + head : H + head + 1, columns]
                product = product + shrink * before_ref[2 * H + head : 2 * H + head + 1, columns]
            stats_ref[head : head + 1, columns] = top
            stats_ref[H + head : H + head + 1, columns] = total
            stats_ref[2 * H + head : 2 * H + head + 1, columns] = product


def first_kernel(cams, blocks, masks, shard_rows, block_keys, span, tile_rows, factor, query_ref, grad_ref, *refs):
    pieces, (chunk_ref, table_ref), outs = refs[:cams], refs[cams : cams + 2], refs[cams + 2 :]
    stats_ref, query_t_ref, grad_t_ref, bias_ref, far_ref, full_table_ref = outs
    rows, _ = query_ref.shape
    own_tiles = rows // tile_rows
    note = slice(2 * rows // cams, 2 * rows // cams + own_tiles)
    full_table_ref[...] = table_ref[...]
    full_table_ref[own_tiles : 2 * own_tiles, :blocks] = pieces[0][note, :blocks]
    build_bias(full_table_ref, bias_ref, masks, shard_rows, block_keys)
    piece_rows = 2 * rows // cams
    for shift in range(cams):
        piece = lax.rem(lax.axis_index("cam") + cams - shift, cams)
        start = pl.multiple_of(piece * piece_rows, 16)
        far_ref[pl.ds(start, piece_rows), :] = pieces[shift][:piece_rows, :]
    query_t_ref[:, :rows] = query_ref[...].T
    query_t_ref[:, rows:] = far_ref[:rows, :].T
    grad_t_ref[:, :rows] = grad_ref[...].T
    grad_t_ref[:, rows:] = far_ref[rows:, :].T
    bias = bias_ref[: chunk_ref.shape[0], :]
    stats_of(chunk_ref, bias, query_t_ref, grad_t_ref, None, stats_ref, span, tile_rows, factor)


def second_kernel(span, tile_rows, factor, chunk_ref, bias_ref, query_t_ref, grad_t_ref, before_ref, stats_ref):
    bias = bias_ref[chunk_ref.shape[0] :, :]
    stats_of(chunk_ref, bias, query_t_ref, grad_t_ref, before_ref, stats_ref, span, tile_rows, factor)


def head_rows(head, width):
    return slice(head * width // H, (head + 1) * width // H)


def staggered(count, stages, lags):
    results = [{} for _ in stages]
    total = sum(lags)
    for n in range(count + total):
        at = n
        for k, stage in enumerate(stages):
            at -= lags[k]
            if 0 <= at < count:
                results[k][at] = stage(at) if k == 0 else stage(at, results[k - 1].pop(at))


def block_list(queries, span):
    return [(head, slice(first, first + span)) for head in range(H) for first in range(0, queries, span)]


def near_kernel(span, tile_rows, factor, near_ref, chunk_ref, held_ref, bias_ref, query_t_ref, grad_t_ref, weights_ref,
                dprobs_ref, keys_t_ref, held_t_ref):
    width, queries = query_t_ref.shape
    keys, values = chunk_of(chunk_ref, width)
    keys_t_ref[...] = chunk_ref[:, :width].T
    held_t_ref[...] = held_ref[:, :width].T
    bias = bias_ref[chunk_ref.shape[0] :, :]
    blocks = block_list(queries, span)

    def terms(n):
        head, columns = blocks[n]
        rows = head_rows(head, width)
        return head_terms(
            head, span, columns.start, tile_rows, keys, values, bias, query_t_ref[rows, columns], grad_t_ref[rows, columns]
        )

    def store(n, raw):
        head, columns = blocks[n]
        place = slice(n * span, (n + 1) * span)
        weights_ref[:, place] = jnp.exp2(raw[0] * factor - near_ref[head : head + 1, columns])
        dprobs_ref[:, place] = raw[1]

    staggered(len(blocks), (terms, store), (0, 1))


def products_of(blocks, queries, query_t_ref, grad_t_ref, keys_t, query_sum_ref, before_ref, out_ref, scale):
    width = query_t_ref.shape[0]
    partial, done = {}, {}

    def products(n, ready):
        head, columns = blocks[n]
        probs, dscores = ready
        rows = head_rows(head, width)
        key_part = dot(query_t_ref[rows, columns], dscores, NT)
        value_part = dot(grad_t_ref[rows, columns], probs, NT)
        piece = dot(keys_t[rows, :], dscores, NN)
        if before_ref is not None:
            piece += before_ref[rows, columns]
        query_sum_ref[rows, columns] = piece
        if columns.start > 0:
            before = partial.pop(head)
            key_part, value_part = before[0] + key_part, before[1] + value_part
        if columns.stop < queries:
            partial[head] = (key_part, value_part)
        else:
            done[head] = (key_part * scale, value_part)
        if rows.stop % LANES == 0 and head in done:
            heads = sorted(done)
            for side in range(2):
                group = jnp.concatenate([done[h][side] for h in heads], axis=0)
                place = side * width + rows.stop - LANES
                out_ref[:, place : place + LANES] = group.T.astype(out_ref.dtype)
            done.clear()

    return products


def third_kernel(span, scale, near_ref, across_ref, keys_t_ref, query_t_ref, grad_t_ref, weights_ref, dprobs_ref,
                 out_ref, query_sum_ref, ends_ref, shrink_ref):
    _, queries = query_t_ref.shape
    rows = queries // 2
    turned = jnp.concatenate((across_ref[:, rows:], across_ref[:, :rows]), axis=1)
    top = jnp.maximum(near_ref[:H, :], turned[:H, :])
    near, across = jnp.exp2(near_ref[:H, :] - top), jnp.exp2(turned[:H, :] - top)
    total = near + across
    lse = top + jnp.log2(total)
    ends_ref[:H, :] = lse
    ends_ref[H:, :] = (near * near_ref[H:, :] + across * turned[H:, :]) / total
    shrink_ref[...] = jnp.exp2(near_ref[:H, :] - lse)
    keys_t = keys_t_ref[...]
    blocks = block_list(queries, span)

    def rounded(n):
        head, columns = blocks[n]
        place = slice(n * span, (n + 1) * span)
        probs = weights_ref[:, place] * shrink_ref[head : head + 1, columns]
        dscores = probs * (dprobs_ref[:, place] - ends_ref[H + head : H + head + 1, columns])
        return probs.astype(BF16), dscores.astype(BF16)

    products = products_of(blocks, queries, query_t_ref, grad_t_ref, keys_t, query_sum_ref, None, out_ref, scale)
    staggered(len(blocks), (rounded, products), (0, 1))


def fourth_kernel(cams, span, tile_rows, factor, scale, ends_ref, before_ref, chunk_ref, keys_t_ref, bias_ref, query_t_ref,
                  grad_t_ref, out_ref, keep_ref, *refs):
    turn_refs, (query_sum_ref, whole_ref) = refs[: cams - 1], refs[cams - 1 :]
    width, queries = query_t_ref.shape
    keys, values = chunk_of(chunk_ref, width)
    keys_t = keys_t_ref[...]
    bias = bias_ref[: chunk_ref.shape[0], :]
    blocks = block_list(queries, span)

    def terms(n):
        head, columns = blocks[n]
        rows = head_rows(head, width)
        return head_terms(
            head, span, columns.start, tile_rows, keys, values, bias, query_t_ref[rows, columns], grad_t_ref[rows, columns]
        )

    def rounded(n, raw):
        head, columns = blocks[n]
        probs = jnp.exp2(raw[0] * factor - ends_ref[head : head + 1, columns])
        dscores = probs * (raw[1] - ends_ref[H + head : H + head + 1, columns])
        return probs.astype(BF16), dscores.astype(BF16)

    products = products_of(blocks, queries, query_t_ref, grad_t_ref, keys_t, query_sum_ref, before_ref, out_ref, scale)
    staggered(len(blocks), (terms, rounded, products), (0, 1, 2))
    count = keep_ref.shape[0] // 2
    if count % LANES:
        whole_ref[...] = query_sum_ref[...].T
    for shift, ref in enumerate((keep_ref, *turn_refs)):
        piece = lax.rem(lax.axis_index("cam") + shift, cams)
        for side in range(2):
            start = pl.multiple_of(side * (queries // 2) + piece * count, count)
            if count % LANES:
                part = whole_ref[pl.ds(start, count), :]
            else:
                part = query_sum_ref[:, pl.ds(start, count)].T
            ref[side * count : (side + 1) * count, :] = (part * scale).astype(ref.dtype)


def run(kernel, outs, args, scratch=(), flops=0, space=pltpu.VMEM):
    size = lambda a: math.prod(a.shape) * a.dtype.itemsize
    moved = sum(size(a) for a in args) + sum(size(a) for a in outs)
    vmem = pl.BlockSpec(memory_space=pltpu.VMEM)
    return pl.pallas_call(
        kernel,
        out_shape=tuple(outs),
        in_specs=[pl.BlockSpec(memory_space=space)] * len(args),
        out_specs=tuple([vmem] * len(outs)),
        scratch_shapes=list(scratch),
        cost_estimate=pl.CostEstimate(flops=flops, bytes_accessed=moved, transcendentals=flops // 64),
        compiler_params=pltpu.CompilerParams(vmem_limit_bytes=40 * 1024 * 1024),
    )(*args)


def combine(parts, factor):
    top = functools.reduce(jnp.maximum, [part[:H] for part in parts])
    shrink = [jnp.exp2((part[:H] - top) * factor) for part in parts]
    total = sum(s * part[H : 2 * H] for s, part in zip(shrink, parts))
    product = sum(s * part[2 * H :] for s, part in zip(shrink, parts))
    return jnp.concatenate((top * factor + jnp.log2(total), product / total), axis=0)


def shards(queries, keys, values, grad_out, visible, counts):
    rows, width = queries.shape
    shard_rows = keys.shape[0]
    head_dim = width // H
    scale = 1.0 / math.sqrt(head_dim)
    factor = scale * math.log2(math.e)
    tiles, cams = lax.axis_size("tile"), lax.axis_size("cam")
    cam = lax.axis_index("cam")
    blocks = counts.shape[0]
    block_keys = shard_rows * tiles // blocks
    own_tiles = visible.shape[0]
    tile_rows = rows // own_tiles
    orders = step_orders(tiles)
    masks = [slot_masks(order) for order in orders]
    span = 256

    def across(x, hop):
        pairs = [(c * tiles + t, c * tiles + (t ^ hop(c))) for c in range(cams) for t in range(tiles)]
        return lax.ppermute(x, ("cam", "tile"), pairs)

    def step(x, k):
        return across(x, lambda c: orders[c % 2][k])

    def swap_half(x):
        return across(x, lambda c: tiles // 2)

    def turn(x, shift):
        return lax.ppermute(x, "cam", [(c, (c + shift) % cams) for c in range(cams)])

    steps = len(orders[0])
    shape = jax.ShapeDtypeStruct
    piece_rows = 2 * rows // cams
    lanes = -(-blocks // LANES) * LANES
    fixed = (keys, values, queries, grad_out, visible, counts.reshape(1, blocks))
    held, query_near, grad_near, message, table = run(
        functools.partial(start_kernel, cams),
        (
            shape((shard_rows, 2 * width), BF16),
            shape((rows, width), BF16),
            shape((rows, width), BF16),
            shape((piece_rows + 16, width), BF16),
            shape((LANES, lanes), BF16),
        ),
        tuple(pltpu.with_memory_space_constraint(x, pltpu.HBM) for x in fixed),
        scratch=(
            pltpu.VMEM(visible.shape, visible.dtype),
            pltpu.VMEM((1, blocks), counts.dtype),
            pltpu.SemaphoreType.DMA((len(fixed),)),
        ),
        space=pltpu.HBM,
    )
    received = swap_half(message)
    for k in range(steps - 2):
        held = jnp.concatenate((held, step(held, k)), axis=0)
    nearer = step(held, steps - 2)
    farther = step(held, steps - 1)
    farthest = across(held, lambda c: orders[c % 2][-1] ^ orders[c % 2][-2])
    pieces = [received] + [turn(received, shift) for shift in range(1, cams)]
    held = jnp.concatenate((held, nearer), axis=0)
    last = jnp.concatenate((farther, farthest), axis=0)

    all_rows = 2 * rows
    chunk = held.shape[0]
    work = 2 * all_rows * chunk * width
    stats, query_t, grad_t, bias = run(
        functools.partial(first_kernel, cams, blocks, masks, shard_rows, block_keys, span, tile_rows, factor),
        (
            shape((3 * H, all_rows), F32),
            shape((width, all_rows), BF16),
            shape((width, all_rows), BF16),
            shape((2 * chunk, LANES), BF16),
        ),
        (query_near, grad_near, *pieces, held, table),
        scratch=(pltpu.VMEM((2 * rows, width), BF16), pltpu.VMEM((LANES, lanes), BF16)),
            flops=8 * work,
    )
    (stats,) = run(
        functools.partial(second_kernel, span, tile_rows, factor),
        (shape((3 * H, all_rows), F32),),
        (last, bias, query_t, grad_t, stats),
        flops=8 * work,
    )
    near = combine([stats] + [turn(stats, shift) for shift in range(1, cams)], factor)
    opposite = swap_half(near)
    weights, dprobs, keys_t, held_t = run(
        functools.partial(near_kernel, span, tile_rows, factor),
        (
            shape((chunk, H * all_rows), F32),
            shape((chunk, H * all_rows), F32),
            shape((width, chunk), BF16),
            shape((width, chunk), BF16),
        ),
        (near, last, held, bias, query_t, grad_t),
        flops=8 * work,
    )

    sent, query_sum, ends = run(
        functools.partial(third_kernel, span, scale),
        (shape((chunk, 2 * width), BF16), shape((width, all_rows), F32), shape((2 * H, all_rows), F32)),
        (near, opposite, keys_t, query_t, grad_t, weights, dprobs),
        scratch=(pltpu.VMEM((H, all_rows), F32),),
        flops=20 * work,
    )
    got = step(sent, steps - 1)
    part = rows // cams
    kept, query_part, *to_turn = run(
        functools.partial(fourth_kernel, cams, span, tile_rows, factor, scale),
        (
            shape((chunk, 2 * width), F32),
            shape((2 * part, width), F32),
            *(shape((2 * part, width), BF16) for _ in range(1, cams)),
        ),
        (ends, query_sum, held, held_t, bias, query_t, grad_t),
        scratch=(pltpu.VMEM((width, all_rows), F32), pltpu.VMEM((all_rows, width), F32)),
            flops=20 * work,
    )
    for shift in range(1, cams):
        query_part = query_part + turn(to_turn[shift - 1], shift).astype(F32)
    query_far = query_part[part:].astype(BF16)
    query_got = swap_half(query_far)
    sums = kept + got.astype(F32)
    slots = [sums[k * shard_rows : (k + 1) * shard_rows] for k in range(chunk // shard_rows)]
    outs = [slot.astype(BF16) for slot in slots[1:]]
    owned = slots[0]
    for k in range(len(outs), 0, -1):
        owned = owned + across(outs[k - 1], lambda c: masks[c % 2][k]).astype(F32)
    owned = owned.astype(BF16)
    mine = (query_part[:part] + query_got.astype(F32)).astype(BF16)
    parts = [mine] + [turn(mine, shift) for shift in range(1, cams)]
    ordered = []
    for k in range(cams):
        source = (cam + cams - k) % cams
        ordered.append(functools.reduce(lambda x, s: jnp.where(source == s, parts[s], x), range(1, cams), parts[0]))
    query_part = jnp.concatenate(ordered, axis=0)
    return (query_part, owned[:, :width], owned[:, width:])


def solution(mesh):
    in_specs = (
        P("tile", None),
        P(("cam", "tile"), None),
        P(("cam", "tile"), None),
        P("tile", None),
        P("tile", "cam"),
        P("cam"),
    )
    out_specs = (P("tile", None), P(("cam", "tile"), None), P(("cam", "tile"), None))

    return jax.shard_map(shards, mesh=mesh, in_specs=in_specs, out_specs=out_specs, check_vma=False)
```
